256 devices in a mesh: bead: 16 (over x, z_lo), slab: 8 (over y, z_hi), grp: 2 (over core).
Axes of the slice: x: 4, y: 4, z: 8 (z_hi: 2, z_lo: 4; z = z_hi * 4 + z_lo), core: 2. Of those that a mesh axis runs over, the one named last changes fastest.
Arguments:
- positions: float32 [64, 3, 65536], P('bead', None, ('slab', 'grp')), may hold values from -6 to 6
- momenta: float32 [64, 3, 65536], P('bead', None, ('slab', 'grp')), may hold values from -12 to 12
- force_old: float32 [64, 3, 65536], P('bead', None, ('slab', 'grp')), may hold values from -6 to 6
- noise: float32 [64, 3, 65536], P('bead', None, ('slab', 'grp')), may hold values from -6 to 6
- mass: float32 [65536], P(('slab', 'grp')), may hold values from 1 to 16
- pair_list: int32 [65536, 32], P(('slab', 'grp')), may hold values from 0 to 4351, as said below
- desc_w: bfloat16 [128, 1600], replicated, may hold values from -0.5 to 0.5
- hidden_one: bfloat16 [1600, 240], replicated, may hold values from -0.15625 to 0.15625
- hidden_two: bfloat16 [240, 240], replicated, may hold values from -0.375 to 0.375
- hidden_three: bfloat16 [240, 240], replicated, may hold values from -0.375 to 0.375
- out_w: bfloat16 [240, 3], replicated, may hold values from -0.375 to 0.375
Outputs:
- new_positions: float32 [64, 3, 65536], P('bead', None, ('slab', 'grp'))
- new_momenta: float32 [64, 3, 65536], P('bead', None, ('slab', 'grp'))
- force_new: float32 [64, 3, 65536], P('bead', None, ('slab', 'grp'))
The draws below stay inside these ranges and needn't reach their ends.
Inputs may be any that keep to these rules, and one draw needn't show every extreme that they name: `pair_list`: for the atom with index li in its slab, every entry lies in li .. li + 256; entries past a count of 16 to 32 per atom name the atom itself, li + 128.
All inputs are finite; a program needn't handle non-finite values.
Results may differ from the reference program's by a relative error of at most 0.00096.
Values sent between devices are 32-bit elements; how exact they have to be, the bound alone decides.
A program may use at most 128 MiB of HBM per device.

```python
import jax
import jax.numpy as jnp
from jax import lax

BEADS = 64
NC = 8
A_SLAB = 4096
K = 32
EDGE = 128
DESC = 1600
HID = 240
ENV = 128
ATOMS = 65536


def draw_pair_list(key, part):
    first_key, second_key = jax.random.split(jax.random.fold_in(key, 11))
    local = jnp.arange(ATOMS, dtype=jnp.int32) % A_SLAB
    offsets = jax.random.randint(first_key, (ATOMS, K), 0, 2 * EDGE + 1).astype(jnp.int32)
    counts = jax.random.randint(second_key, (ATOMS, 1), K // 2, K + 1).astype(jnp.int32)
    slot = jnp.arange(K, dtype=jnp.int32)[None, :]
    offsets = jnp.where((local[:, None] == A_SLAB - 1) & (slot == 0), 2 * EDGE, offsets)
    offsets = jnp.where((local[:, None] == 0) & (slot == 0), 0, offsets)
    picked = local[:, None] + offsets
    itself = local[:, None] + EDGE
    return jnp.where(slot < counts, picked, itself).astype(jnp.int32)


def block_scale(rng, shape, cuts, smallest, high):
    level = 1.0
    for axis_at, parts in cuts:
        draws = jax.random.uniform(jax.random.fold_in(jax.random.fold_in(rng, 6), axis_at), (parts,), jnp.float32, smallest / len(cuts), high / len(cuts))
        level = level * jnp.repeat(jnp.exp(draws), shape[axis_at] // parts).reshape((-1,) + (1,) * (len(shape) - 1 - axis_at))
    return level


def bell_draw(rng, dims, deviation, most, shards=(), held_as=jnp.bfloat16):
    gain = block_scale(rng, dims, shards, -0.22, 0.18) if shards else 1.0
    result = jax.random.normal(rng, dims, jnp.float32) * deviation * gain
    return jnp.minimum(jnp.maximum(result, -most), most).astype(held_as)


def setup_inputs(seed: int = 0) -> dict:
    keys = jax.random.split(jax.random.key(seed), 12)
    return {
        "positions": bell_draw(keys[0], (BEADS, 3, ATOMS), 1.0, 6.0, ((0, 16), (2, 16)), jnp.float32),
        "momenta": bell_draw(keys[1], (BEADS, 3, ATOMS), 2.0, 12.0, ((0, 16), (2, 16)), jnp.float32),
        "force_old": bell_draw(keys[2], (BEADS, 3, ATOMS), 1.0, 6.0, ((0, 16), (2, 16)), jnp.float32),
        "noise": bell_draw(keys[3], (BEADS, 3, ATOMS), 1.0, 6.0, ((0, 16), (2, 16)), jnp.float32),
        "mass": jnp.clip(1.0 + 15.0 * jax.random.uniform(keys[4], (ATOMS,), jnp.float32) ** block_scale(keys[4], (ATOMS,), ((0, 16),), -0.2, 0.2), 1.0, 16.0),
        "pair_list": draw_pair_list(jax.random.fold_in(keys[11], 71), 0),
        "desc_w": bell_draw(keys[6], (ENV, DESC), ENV ** -0.5, 0.5),
        "hidden_one": bell_draw(keys[7], (DESC, HID), DESC ** -0.5, 0.15625),
        "hidden_two": bell_draw(keys[8], (HID, HID), HID ** -0.5, 0.375),
        "hidden_three": bell_draw(keys[9], (HID, HID), HID ** -0.5, 0.375),
        "out_w": bell_draw(keys[10], (HID, 3), HID ** -0.5, 0.375),
    }


TIME_STEP = 0.1
CYCLE_FREQ = 5.0
CENTROID_FRICTION = 1.0
PAIR_STRENGTH = 0.5

def cycle_tables(beads, contracted):
    index = jnp.arange(beads, dtype=jnp.float32)
    mode_int = jnp.arange(beads, dtype=jnp.int32)[None, :]
    angle = 2.0 * jnp.pi * index[:, None] * index[None, :] / beads
    half_mode = beads // 2
    root_one = 1.0 / jnp.sqrt(jnp.float32(beads))
    root_two = jnp.sqrt(2.0 / jnp.float32(beads))
    basis = jnp.where(mode_int == 0, root_one * jnp.ones_like(angle), jnp.where(mode_int < half_mode, root_two * jnp.cos(angle), jnp.where(mode_int == half_mode, root_one * jnp.cos(angle), root_two * jnp.sin(angle))))
    freq = 2.0 * CYCLE_FREQ * jnp.sin(jnp.pi * index / beads)
    cindex = jnp.arange(contracted, dtype=jnp.float32)
    spacing = index[None, :] / beads - cindex[:, None] / contracted
    kernel = jnp.ones_like(spacing)
    for order in range(1, contracted // 2):
        kernel = kernel + 2.0 * jnp.cos(2.0 * jnp.pi * order * spacing)
    kernel = kernel + jnp.cos(jnp.pi * contracted * spacing)
    return (basis, freq, kernel / beads)

def free_drift(modes_q, modes_p, freq, masses):
    step = 0.5 * TIME_STEP
    rate = freq[:, None, None]
    moving = rate > 0.0
    safe = jnp.where(moving, rate, 1.0)
    cosine = jnp.cos(safe * step)
    sine = jnp.sin(safe * step)
    new_q = jnp.where(moving, cosine * modes_q + sine / (masses * safe) * modes_p, modes_q + step * modes_p / masses)
    new_p = jnp.where(moving, cosine * modes_p - masses * safe * sine * modes_q, modes_p)
    return (new_q, new_p)

def thermostat(modes_p, noise, freq, masses):
    friction = jnp.where(freq > 0.0, 2.0 * freq, CENTROID_FRICTION)
    keep = jnp.exp(-friction * TIME_STEP)[:, None, None]
    return keep * modes_p + jnp.sqrt(masses) * jnp.sqrt(1.0 - keep * keep) * noise

def wide_dot(left, right):
    return jnp.dot(left.astype(jnp.float32), right.astype(jnp.float32), precision=lax.Precision.HIGHEST, preferred_element_type=jnp.float32)

def neural_force(extended, lists, start, weights):
    desc_w, hidden_one, hidden_two, hidden_three, out_w = weights
    count = lists.shape[0]
    near = extended[:, lists]
    own = lax.dynamic_slice_in_dim(extended, start + EDGE, count, 1)[:, :, None]
    apart = near - own
    closeness = 1.0 / (1.0 + lax.optimization_barrier(jnp.sum(apart * apart, axis=0)))
    env = jnp.concatenate([apart, closeness[None]], axis=0)
    env = jnp.transpose(env, (1, 2, 0)).reshape(count, -1).astype(jnp.bfloat16)
    layer = jnp.tanh(wide_dot(env, desc_w)).astype(jnp.bfloat16)
    for matrix in (hidden_one, hidden_two, hidden_three):
        layer = jnp.tanh(wide_dot(layer, matrix)).astype(jnp.bfloat16)
    return wide_dot(layer, out_w).T

def contracted_forces(extended, lists, start, weights):

    def one_bead(single):
        return neural_force(single, lists, start, weights)
    return lax.map(one_bead, extended)

def pair_force(extended_one, lists):
    near = extended_one[:, lists]
    own = extended_one[:, EDGE:EDGE + lists.shape[0]][:, :, None]
    apart = near - own
    closeness = 1.0 / (1.0 + lax.optimization_barrier(jnp.sum(apart * apart, axis=0, keepdims=True)))
    return PAIR_STRENGTH * lax.optimization_barrier(jnp.sum(apart * closeness, axis=2))

def slab_extend(field):
    lead = field.shape[0]
    slabs = jnp.transpose(field.reshape(lead, 3, -1, A_SLAB), (2, 0, 1, 3))
    before = jnp.roll(slabs, 1, axis=0)[..., A_SLAB - EDGE:]
    after = jnp.roll(slabs, -1, axis=0)[..., :EDGE]
    return jnp.concatenate([before, slabs, after], axis=3)

def reference(positions, momenta, force_old, noise, mass, pair_list, desc_w, hidden_one, hidden_two, hidden_three, out_w):
    best = lax.Precision.HIGHEST
    basis, freq, contract = cycle_tables(BEADS, NC)
    masses = mass[None, None, :]
    kicked = momenta + 0.5 * TIME_STEP * force_old
    modes_q = jnp.einsum('bk,bxa->kxa', basis, positions, precision=best)
    modes_p = jnp.einsum('bk,bxa->kxa', basis, kicked, precision=best)
    modes_q, modes_p = free_drift(modes_q, modes_p, freq, masses)
    modes_p = thermostat(modes_p, noise, freq, masses)
    modes_q, modes_p = free_drift(modes_q, modes_p, freq, masses)
    new_q = jnp.einsum('bk,kxa->bxa', basis, modes_q, precision=best)
    moved = jnp.einsum('bk,kxa->bxa', basis, modes_p, precision=best)
    contracted = jnp.einsum('cb,bxa->cxa', contract, new_q, precision=best)
    slab_lists = pair_list.reshape(-1, A_SLAB, K)
    weights = (desc_w, hidden_one, hidden_two, hidden_three, out_w)

    def slab_neural(pieces):
        extended, lists = pieces
        return contracted_forces(extended, lists, jnp.int32(0), weights)
    neural = lax.map(slab_neural, (slab_extend(contracted), slab_lists))
    neural = jnp.transpose(neural, (1, 2, 0, 3)).reshape(NC, 3, -1)
    spread = BEADS / NC * jnp.einsum('cb,cxa->bxa', contract, neural, precision=best)

    def slab_pair(pieces):
        extended, lists = pieces

        def one_bead(single):
            return pair_force(single, lists)
        return lax.map(one_bead, extended)
    pairs = lax.map(slab_pair, (slab_extend(new_q), slab_lists))
    pairs = jnp.transpose(pairs, (1, 2, 0, 3)).reshape(BEADS, 3, -1)
    force_new = pairs + spread
    return (new_q, moved + 0.5 * TIME_STEP * force_new, force_new)
```

```python
import functools

import jax
import jax.numpy as jnp
import numpy as np
from jax import lax
from jax.experimental import pallas as pl
from jax.experimental.pallas import tpu as pltpu
from jax.sharding import PartitionSpec as P

BEADS = 64
NC = 8
LANE = 128
TIME_STEP = 0.1
CYCLE_FREQ = 5.0
CENTROID_FRICTION = 1.0
PAIR_STRENGTH = 0.5
MESH = pl.DeviceIdType.MESH


def cycle_tables(beads, contracted):
    index = np.arange(beads, dtype=np.float64)
    mode = np.arange(beads)[None, :]
    angle = 2.0 * np.pi * index[:, None] * index[None, :] / beads
    half = beads // 2
    root_one = 1.0 / np.sqrt(beads)
    root_two = np.sqrt(2.0 / beads)
    alternate = np.where(np.arange(beads) % 2 == 0, 1.0, -1.0)[:, None]
    basis = np.where(
        mode == 0,
        root_one,
        np.where(
            mode < half,
            root_two * np.cos(angle),
            np.where(mode == half, root_one * alternate, root_two * np.sin(angle)),
        ),
    )
    freq = 2.0 * CYCLE_FREQ * np.sin(np.pi * index / beads)
    spacing = index[None, :] / beads - np.arange(contracted)[:, None] / contracted
    kernel = np.ones_like(spacing)
    for order in range(1, contracted // 2):
        kernel = kernel + 2.0 * np.cos(2.0 * np.pi * order * spacing)
    kernel = kernel + np.cos(np.pi * contracted * spacing)
    return basis, freq, kernel / beads


def step_tables(beads, contracted):
    basis, freq, contract = cycle_tables(beads, contracted)
    step = 0.5 * TIME_STEP
    moving = freq > 0.0
    safe = np.where(moving, freq, 1.0)
    cos = np.where(moving, np.cos(safe * step), 1.0)
    sin_over = np.where(moving, np.sin(safe * step) / safe, step)
    sin_times = np.where(moving, np.sin(safe * step) * safe, 0.0)
    keep = np.exp(-np.where(moving, 2.0 * freq, CENTROID_FRICTION) * TIME_STEP)
    kick = np.sqrt(1.0 - keep * keep)

    def both(diag):
        return (basis * diag[None, :]) @ basis.T

    q_rows = np.concatenate(
        [
            both(cos * cos - keep * sin_over * sin_times),
            both(cos * sin_over * (1.0 + keep)),
            basis * (sin_over * kick)[None, :],
        ],
        axis=1,
    )
    p_rows = np.concatenate(
        [
            both(-cos * sin_times * (1.0 + keep)),
            both(cos * cos * keep - sin_over * sin_times),
            basis * (cos * kick)[None, :],
        ],
        axis=1,
    )
    return np.concatenate([q_rows, p_rows, contract @ q_rows], axis=0), contract


def split_table(table):
    table = jnp.asarray(table.astype(np.float32))
    high = table.astype(jnp.bfloat16)
    low = (table - high.astype(jnp.float32)).astype(jnp.bfloat16)
    return high, low


def dot32(left, right):
    return jnp.dot(left, right, preferred_element_type=jnp.float32)


def table_dot(high, low, x):
    x_high = x.astype(jnp.bfloat16)
    x_low = (x - x_high.astype(jnp.float32)).astype(jnp.bfloat16)
    return dot32(high, x_high) + (dot32(high, x_low) + dot32(low, x_high))


def near_minus_own(rows, low, first, third):
    got = [
        jnp.take_along_axis(
            jnp.broadcast_to(row, low.shape), low, axis=1, mode="promise_in_bounds"
        )
        for row in rows
    ]
    near = jnp.where(first, got[0], jnp.where(third, got[2], got[1]))
    return near - rows[1]


def tile_lists(list_ref, tile):
    index = list_ref[:, pl.ds(pl.multiple_of(tile * LANE, LANE), LANE)] - tile * LANE
    return index & (LANE - 1), index < LANE, index >= 2 * LANE


def kernel(
    groups,
    q_hbm,
    n_hbm,
    p_hbm,
    f_hbm,
    mass_hbm,
    list_hbm,
    desc_hbm,
    one_hbm,
    two_hbm,
    three_hbm,
    out_w_hbm,
    perm_hbm,
    w_high_hbm,
    w_low_hbm,
    s_high_hbm,
    s_low_hbm,
    out_q,
    out_m,
    out_f,
    p_ref,
    f_ref,
    mass_ref,
    two_ref,
    three_ref,
    out_w_ref,
    perm_ref,
    w_high,
    w_low,
    s_high,
    s_low,
    kick_buf,
    recv_in,
    xs,
    y_buf,
    back,
    ext,
    neural,
    s_buf,
    s_recv,
    pair_buf,
    lists,
    desc,
    desc_p,
    one,
    local_sem,
    own_sem,
    in_send,
    in_recv,
    y_send,
    y_recv,
    s_send,
    s_recv_sem,
    halo_send,
    halo_recv,
    edge_send,
    edge_recv,
):
    nb = groups
    bl = p_ref.shape[1]
    last = p_ref.shape[2]
    block = p_ref.shape[2] // nb
    tiles = p_ref.shape[2] // LANE
    wide = block // LANE
    beads = nb * bl
    nc = ext.shape[1]
    me = lax.axis_index("bead")
    slabs, cores = lax.axis_size("slab"), lax.axis_size("grp")
    total = slabs * cores
    slab = lax.axis_index("slab") * cores + lax.axis_index("grp")

    def device(place, at):
        return {"bead": place, "slab": at // cores, "grp": at % cores}

    up, down = (slab + 1) % total, (slab + total - 1) % total
    after = device((me + 1) % nb, (slab + (me + 1) // nb) % total)
    before = device((me + nb - 1) % nb, (slab + total - 1 + (me + nb - 1) // nb) % total)

    moves = (
        (p_hbm, p_ref),
        (f_hbm, f_ref),
        (desc_hbm, desc),
        (perm_hbm, perm_ref),
        (mass_hbm, mass_ref),
        (w_high_hbm, w_high),
        (w_low_hbm, w_low),
        (list_hbm, lists),
        (one_hbm, one),
        (two_hbm, two_ref),
        (three_hbm, three_ref),
        (out_w_hbm, out_w_ref),
        (s_high_hbm, s_high),
        (s_low_hbm, s_low),
    )
    loads = [
        pltpu.make_async_copy(source, dest, local_sem.at[at])
        for at, (source, dest) in enumerate(moves)
    ]
    for load in loads:
        load.start()

    barrier = pltpu.get_barrier_semaphore()

    def greet(off, carry):
        pl.semaphore_signal(
            barrier, inc=1, device_id=device((me + off) % nb, slab), device_id_type=MESH
        )
        return carry

    lax.fori_loop(1, nb, greet, 0)
    for other in (device(me, up), device(me, down), before, after):
        pl.semaphore_signal(barrier, inc=1, device_id=other, device_id_type=MESH)
    for load in loads[:2]:
        load.wait()
    kick_buf[...] = p_ref[...] + 0.5 * TIME_STEP * f_ref[...]
    pl.semaphore_wait(barrier, nb - 1 + 4)

    def lanes_of(place):
        return pl.ds(pl.multiple_of(place * block, LANE), block)

    sources = (q_hbm, n_hbm, kick_buf)

    def send_in(which, dest, source):
        return pltpu.make_async_remote_copy(
            src_ref=sources[which].at[:, :, lanes_of(dest)],
            dst_ref=recv_in.at[which, source],
            send_sem=in_send.at[which, dest],
            recv_sem=in_recv.at[which, source],
            device_id=device(dest, slab),
            device_id_type=MESH,
        )

    def start_in(off, carry):
        for which in range(3):
            send_in(which, (me + off) % nb, me).start()
        return carry

    lax.fori_loop(1, nb, start_in, 0)
    owns = [
        pltpu.make_async_copy(
            sources[which].at[:, :, lanes_of(me)], recv_in.at[which, me], own_sem.at[which]
        )
        for which in range(3)
    ]
    for own in owns:
        own.start()

    for load in loads[2:]:
        load.wait()
    desc_p[...] = dot32(desc[...], perm_ref[...]).astype(jnp.bfloat16)

    for own in owns:
        own.wait()

    def wait_in(off, carry):
        for which in range(3):
            send_in(which, (me + off) % nb, (me + off) % nb).wait_recv()
        return carry

    lax.fori_loop(1, nb, wait_in, 0)

    for which, part in ((0, 0), (2, 1), (1, 2)):
        for place in range(nb):
            for comp in range(3):
                row = part * beads + place * bl
                xs[row : row + bl, comp * block : (comp + 1) * block] = recv_in[which, place, comp]
    heavy = jnp.concatenate(
        [mass_ref[pl.ds(me * wide + h, 1), :] for h in range(wide)] * 3, axis=1
    )
    x_all = jnp.concatenate(
        [
            xs[0:beads, :],
            xs[beads : 2 * beads, :] / heavy,
            xs[2 * beads : 3 * beads, :] / jnp.sqrt(heavy),
        ],
        axis=0,
    )
    y_all = table_dot(w_high[...], w_low[...], x_all)
    contracted = y_all[2 * beads : 2 * beads + nc]
    for comp in range(3):
        for cb in range(nc):
            ext[comp, cb, :, LANE : LANE + block] = contracted[
                cb : cb + 1, comp * block : (comp + 1) * block
            ]
    y_new = y_all[0:beads]
    y_mom = y_all[beads : 2 * beads] * heavy
    for arr, value in ((0, y_new), (1, y_mom)):
        for place in range(nb):
            for comp in range(3):
                y_buf[arr, place, comp] = value[
                    place * bl : (place + 1) * bl, comp * block : (comp + 1) * block
                ]

    far = LANE + block
    halos = [
        pltpu.make_async_remote_copy(
            src_ref=ext.at[:, :, :, pl.ds(block, LANE)],
            dst_ref=ext.at[:, :, :, pl.ds(0, LANE)],
            send_sem=halo_send.at[0],
            recv_sem=halo_recv.at[0],
            device_id=after,
            device_id_type=MESH,
        ),
        pltpu.make_async_remote_copy(
            src_ref=ext.at[:, :, :, pl.ds(LANE, LANE)],
            dst_ref=ext.at[:, :, :, pl.ds(far, LANE)],
            send_sem=halo_send.at[1],
            recv_sem=halo_recv.at[1],
            device_id=before,
            device_id_type=MESH,
        ),
    ]
    for halo in halos:
        halo.start()

    def back_lanes(source):
        return pl.ds(pl.multiple_of(LANE + source * block, LANE), block)

    def send_y(arr, dest, source):
        return pltpu.make_async_remote_copy(
            src_ref=y_buf.at[arr, dest],
            dst_ref=back.at[arr, :, :, back_lanes(source)],
            send_sem=y_send.at[arr, dest],
            recv_sem=y_recv.at[arr, source],
            device_id=device(dest, slab),
            device_id_type=MESH,
        )

    for arr in range(2):

        def start_y(off, carry, arr=arr):
            send_y(arr, (me + off) % nb, me).start()
            return carry

        lax.fori_loop(1, nb, start_y, 0)
    y_own = [
        pltpu.make_async_copy(
            y_buf.at[arr, me], back.at[arr, :, :, back_lanes(me)], own_sem.at[arr]
        )
        for arr in range(2)
    ]
    for own in y_own:
        own.start()
    for halo in halos:
        halo.wait_recv()

    chunk = 512
    depth = one.shape[1]

    def one_contracted(cb, carry):
        env = []
        for h in range(wide):
            low, first, third = tile_lists(lists, me * wide + h)
            apart = []
            for comp in range(3):
                rows = [
                    ext[comp, cb, :, (h + k) * LANE : (h + k + 1) * LANE] for k in range(3)
                ]
                apart.append(near_minus_own(rows, low, first, third))
            close = 1.0 / (
                1.0 + (apart[0] * apart[0] + apart[1] * apart[1] + apart[2] * apart[2])
            )
            env.append(jnp.concatenate(apart + [close], axis=0).astype(jnp.bfloat16))
        env = jnp.concatenate(env, axis=1)
        total_one = None
        for low_at in range(0, depth, chunk):
            high_at = min(low_at + chunk, depth)
            piece = jnp.tanh(dot32(desc_p[low_at:high_at, :], env)).astype(jnp.bfloat16)
            term = dot32(one[:, low_at:high_at], piece)
            total_one = term if total_one is None else total_one + term
        layer = jnp.tanh(total_one).astype(jnp.bfloat16)
        for matrix in (two_ref, three_ref):
            layer = jnp.tanh(
                lax.dot_general(
                    matrix[...],
                    layer,
                    (((0,), (0,)), ((), ())),
                    preferred_element_type=jnp.float32,
                )
            ).astype(jnp.bfloat16)
        force = dot32(out_w_ref[...], layer)
        neural[cb] = force
        return carry

    lax.fori_loop(0, nc, one_contracted, 0)

    for comp in range(3):
        rows = jnp.concatenate([neural[cb, comp : comp + 1, :] for cb in range(nc)], axis=0)
        spread = table_dot(s_high[...], s_low[...], rows)
        for place in range(nb):
            s_buf[place, comp] = spread[place * bl : (place + 1) * bl, :]

    def send_s(dest, source):
        return pltpu.make_async_remote_copy(
            src_ref=s_buf.at[dest],
            dst_ref=s_recv.at[:, :, lanes_of(source)],
            send_sem=s_send.at[dest],
            recv_sem=s_recv_sem.at[source],
            device_id=device(dest, slab),
            device_id_type=MESH,
        )

    def start_s(off, carry):
        send_s((me + off) % nb, me).start()
        return carry

    lax.fori_loop(1, nb, start_s, 0)
    s_own = pltpu.make_async_copy(s_buf.at[me], s_recv.at[:, :, lanes_of(me)], own_sem.at[2])
    s_own.start()

    for own in y_own:
        own.wait()
    for arr in range(2):

        def wait_y(off, carry, arr=arr):
            send_y(arr, (me + off) % nb, (me + off) % nb).wait_recv()
            return carry

        lax.fori_loop(1, nb, wait_y, 0)

    edges = [
        pltpu.make_async_remote_copy(
            src_ref=back.at[0, :, :, pl.ds(last, LANE)],
            dst_ref=back.at[0, :, :, pl.ds(0, LANE)],
            send_sem=edge_send.at[0],
            recv_sem=edge_recv.at[0],
            device_id=device(me, up),
            device_id_type=MESH,
        ),
        pltpu.make_async_remote_copy(
            src_ref=back.at[0, :, :, pl.ds(LANE, LANE)],
            dst_ref=back.at[0, :, :, pl.ds(last + LANE, LANE)],
            send_sem=edge_send.at[1],
            recv_sem=edge_recv.at[1],
            device_id=device(me, down),
            device_id_type=MESH,
        ),
    ]
    for edge in edges:
        edge.start()

    def one_tile(tile, carry):
        low, first, third = tile_lists(lists, tile)
        at = [pl.ds(pl.multiple_of((tile + k) * LANE, LANE), LANE) for k in range(3)]
        sums = [[], [], []]
        for bead in range(bl):
            apart = []
            for comp in range(3):
                rows = [back[0, comp, bead : bead + 1, at[k]] for k in range(3)]
                apart.append(near_minus_own(rows, low, first, third))
            close = PAIR_STRENGTH / (
                1.0 + (apart[0] * apart[0] + apart[1] * apart[1] + apart[2] * apart[2])
            )
            for comp in range(3):
                sums[comp].append(jnp.sum(apart[comp] * close, axis=0, keepdims=True))
        for comp in range(3):
            pair_buf[comp, :, at[0]] = jnp.concatenate(sums[comp], axis=0)
        return carry

    lax.fori_loop(1, tiles - 1, one_tile, 0)
    for edge in edges:
        edge.wait_recv()

    def outer_tile(which, carry):
        return one_tile(which * (tiles - 1), carry)

    lax.fori_loop(0, 2, outer_tile, 0)

    s_own.wait()

    def wait_s(off, carry):
        send_s((me + off) % nb, (me + off) % nb).wait_recv()
        return carry

    lax.fori_loop(1, nb, wait_s, 0)
    force = pair_buf[...] + s_recv[...]
    out_f[...] = force
    out_m[...] = back[1, :, :, LANE : LANE + last] + 0.5 * TIME_STEP * force
    out_q[...] = back[0, :, :, LANE : LANE + last]

    def drain(off, carry):
        dest = (me + off) % nb
        for which in range(3):
            send_in(which, dest, me).wait_send()
        for arr in range(2):
            send_y(arr, dest, me).wait_send()
        send_s(dest, me).wait_send()
        return carry

    lax.fori_loop(1, nb, drain, 0)
    for copy in halos + edges:
        copy.wait_send()


def body(
    positions,
    momenta,
    force_old,
    noise,
    mass,
    pair_list,
    desc_w,
    hidden_one,
    hidden_two,
    hidden_three,
    out_w,
):
    nb = lax.axis_size("bead")
    bl, _, atoms = positions.shape
    beads = nb * bl
    block = atoms // nb
    width = pair_list.shape[1]
    env, wide = desc_w.shape
    hid = hidden_one.shape[1]
    table, contract = step_tables(beads, NC)
    w_high, w_low = split_table(table)
    s_high, s_low = split_table(contract.T * (beads / NC))
    perm = np.zeros((env, env), np.float32)
    for j in range(width):
        for entry in range(4):
            perm[4 * j + entry, entry * width + j] = 1.0
    perm = jnp.asarray(perm, jnp.bfloat16)

    def flip(x):
        return jnp.transpose(x, (1, 0, 2))

    out = jax.ShapeDtypeStruct((3, bl, atoms), jnp.float32)
    f32, bf16 = jnp.float32, jnp.bfloat16
    dma = pltpu.SemaphoreType.DMA
    new_q, new_m, new_f = pl.pallas_call(
        functools.partial(kernel, nb),
        out_shape=(out, out, out),
        in_specs=[pl.BlockSpec(memory_space=pltpu.HBM)] * 16,
        out_specs=(pl.BlockSpec(memory_space=pltpu.VMEM),) * 3,
        scratch_shapes=[
            pltpu.VMEM((3, bl, atoms), f32),
            pltpu.VMEM((3, bl, atoms), f32),
            pltpu.VMEM((atoms // LANE, LANE), f32),
            pltpu.VMEM((hid, hid), bf16),
            pltpu.VMEM((hid, hid), bf16),
            pltpu.VMEM((3, hid), bf16),
            pltpu.VMEM((env, env), bf16),
            pltpu.VMEM(w_high.shape, bf16),
            pltpu.VMEM(w_low.shape, bf16),
            pltpu.VMEM(s_high.shape, bf16),
            pltpu.VMEM(s_low.shape, bf16),
            pltpu.VMEM((3, bl, atoms), f32),
            pltpu.VMEM((3, nb, 3, bl, block), f32),
            pltpu.VMEM((3 * beads, 3 * block), f32),
            pltpu.VMEM((2, nb, 3, bl, block), f32),
            pltpu.VMEM((2, 3, bl, atoms + 2 * LANE), f32),
            pltpu.VMEM((3, NC, 1, block + 2 * LANE), f32),
            pltpu.VMEM((NC, 3, block), f32),
            pltpu.VMEM((nb, 3, bl, block), f32),
            pltpu.VMEM((3, bl, atoms), f32),
            pltpu.VMEM((3, bl, atoms), f32),
            pltpu.VMEM((width, atoms), jnp.int32),
            pltpu.VMEM((wide, env), bf16),
            pltpu.VMEM((wide, env), bf16),
            pltpu.VMEM((hid, wide), bf16),
            dma((14,)),
            dma((3,)),
            dma((3, nb)),
            dma((3, nb)),
            dma((2, nb)),
            dma((2, nb)),
            dma((nb,)),
            dma((nb,)),
            dma((2,)),
            dma((2,)),
            dma((2,)),
            dma((2,)),
        ],
        compiler_params=pltpu.CompilerParams(
            collective_id=0, has_side_effects=True, vmem_limit_bytes=66519040
        ),
    )(
        flip(positions),
        flip(noise),
        flip(momenta),
        flip(force_old),
        mass.reshape(atoms // LANE, LANE),
        pair_list.T,
        desc_w.T,
        hidden_one.T,
        hidden_two,
        hidden_three,
        out_w.T,
        perm,
        w_high,
        w_low,
        s_high,
        s_low,
    )
    return flip(new_q), flip(new_m), flip(new_f)


def solution(mesh):
    whole = P("bead", None, ("slab", "grp"))
    placed = (whole,) * 4 + (P(("slab", "grp")), P(("slab", "grp"), None)) + (P(),) * 5
    return jax.shard_map(
        body, mesh=mesh, in_specs=placed, out_specs=(whole,) * 3, check_vma=False
    )
```

```python
import functools

import jax
import jax.numpy as jnp
import numpy as np
from jax import lax
from jax.experimental import pallas as pl
from jax.experimental.pallas import tpu as pltpu
from jax.sharding import PartitionSpec as P

BEADS = 64
NC = 8
LANE = 128
TIME_STEP = 0.1
CYCLE_FREQ = 5.0
CENTROID_FRICTION = 1.0
PAIR_STRENGTH = 0.5
MESH = pl.DeviceIdType.MESH


def cycle_tables(beads, contracted):
    index = np.arange(beads, dtype=np.float64)
    mode = np.arange(beads)[None, :]
    angle = 2.0 * np.pi * index[:, None] * index[None, :] / beads
    half = beads // 2
    root_one = 1.0 / np.sqrt(beads)
    root_two = np.sqrt(2.0 / beads)
    alternate = np.where(np.arange(beads) % 2 == 0, 1.0, -1.0)[:, None]
    basis = np.where(
        mode == 0,
        root_one,
        np.where(
            mode < half,
            root_two * np.cos(angle),
            np.where(mode == half, root_one * alternate, root_two * np.sin(angle)),
        ),
    )
    freq = 2.0 * CYCLE_FREQ * np.sin(np.pi * index / beads)
    spacing = index[None, :] / beads - np.arange(contracted)[:, None] / contracted
    kernel = np.ones_like(spacing)
    for order in range(1, contracted // 2):
        kernel = kernel + 2.0 * np.cos(2.0 * np.pi * order * spacing)
    kernel = kernel + np.cos(np.pi * contracted * spacing)
    return basis, freq, kernel / beads


def step_tables(beads, contracted):
    basis, freq, contract = cycle_tables(beads, contracted)
    step = 0.5 * TIME_STEP
    moving = freq > 0.0
    safe = np.where(moving, freq, 1.0)
    cos = np.where(moving, np.cos(safe * step), 1.0)
    sin_over = np.where(moving, np.sin(safe * step) / safe, step)
    sin_times = np.where(moving, np.sin(safe * step) * safe, 0.0)
    keep = np.exp(-np.where(moving, 2.0 * freq, CENTROID_FRICTION) * TIME_STEP)
    kick = np.sqrt(1.0 - keep * keep)

    def both(diag):
        return (basis * diag[None, :]) @ basis.T

    q_rows = np.concatenate(
        [
            both(cos * cos - keep * sin_over * sin_times),
            both(cos * sin_over * (1.0 + keep)),
            basis * (sin_over * kick)[None, :],
        ],
        axis=1,
    )
    p_rows = np.concatenate(
        [
            both(-cos * sin_times * (1.0 + keep)),
            both(cos * cos * keep - sin_over * sin_times),
            basis * (cos * kick)[None, :],
        ],
        axis=1,
    )
    return np.concatenate([q_rows, p_rows, contract @ q_rows], axis=0), contract


def split_table(table):
    table = jnp.asarray(table.astype(np.float32))
    high = table.astype(jnp.bfloat16)
    low = (table - high.astype(jnp.float32)).astype(jnp.bfloat16)
    return high, low


def dot32(left, right):
    return jnp.dot(left, right, preferred_element_type=jnp.float32)


def table_dot(high, low, x):
    x_high = x.astype(jnp.bfloat16)
    x_low = (x - x_high.astype(jnp.float32)).astype(jnp.bfloat16)
    return dot32(high, x_high) + (dot32(high, x_low) + dot32(low, x_high))


def gather_near(rows, low, first, third):
    got = [
        jnp.take_along_axis(
            jnp.broadcast_to(row, low.shape), low, axis=1, mode="promise_in_bounds"
        )
        for row in rows
    ]
    return jnp.where(first, got[0], jnp.where(third, got[2], got[1])) - rows[1]


def tile_lists(list_ref, tile, group):
    lanes = pl.ds(pl.multiple_of(tile * LANE, LANE), LANE)
    index = list_ref[8 * group : 8 * group + 8, lanes] - tile * LANE
    return index & (LANE - 1), index < LANE, index >= 2 * LANE


def closeness(apart, scale):
    return scale / (1.0 + (apart[0] * apart[0] + apart[1] * apart[1] + apart[2] * apart[2]))


def kernel(
    groups,
    q_hbm,
    n_hbm,
    p_hbm,
    f_hbm,
    mass_hbm,
    list_hbm,
    desc_hbm,
    one_hbm,
    two_hbm,
    three_hbm,
    out_w_hbm,
    perm_hbm,
    w_high_hbm,
    w_low_hbm,
    s_high_hbm,
    s_low_hbm,
    out_q,
    out_m,
    out_f,
    p_ref,
    f_ref,
    mass_ref,
    two_ref,
    three_ref,
    out_w_ref,
    perm_ref,
    w_high,
    w_low,
    s_high,
    s_low,
    kick_buf,
    recv_in,
    xs,
    y_buf,
    back,
    ext,
    neural,
    s_buf,
    s_recv,
    pair_buf,
    lists,
    desc,
    desc_p,
    one,
    two_t,
    three_t,
    env_buf,
    local_sem,
    own_sem,
    in_send,
    in_recv,
    y_send,
    y_recv,
    s_send,
    s_recv_sem,
    halo_send,
    halo_recv,
    edge_send,
    edge_recv,
):
    nb = groups
    bl = p_ref.shape[1]
    last = p_ref.shape[2]
    block = p_ref.shape[2] // nb
    tiles = p_ref.shape[2] // LANE
    wide = block // LANE
    beads = nb * bl
    nc = ext.shape[1]
    me = lax.axis_index("bead")
    slabs, cores = lax.axis_size("slab"), lax.axis_size("grp")
    total = slabs * cores
    slab = lax.axis_index("slab") * cores + lax.axis_index("grp")

    def device(place, at):
        return {"bead": place, "slab": at // cores, "grp": at % cores}

    up, down = (slab + 1) % total, (slab + total - 1) % total

    def block_of(place, at=slab):
        if nb != 16:
            return place
        core, shift = at % cores, (3 * (at // cores)) % 4
        x, z = (place // 4 + 4 - shift) % 4, place % 4
        along_x = 4 * z + x + (z % 2) * (3 - 2 * x)
        along_z = 4 * x + 3 - z + (x % 2) * (2 * z - 3)
        return along_x + core * (along_z - along_x)

    def place_of(number, at):
        if nb != 16:
            return number
        core, shift = at % cores, (3 * (at // cores)) % 4
        far, near = number // 4, number % 4
        x_first = 4 * ((near + (far % 2) * (3 - 2 * near) + shift) % 4) + far
        z_first = 4 * ((far + shift) % 4) + 3 - near + (far % 2) * (2 * near - 3)
        return x_first + core * (z_first - x_first)

    mine = block_of(me)

    def beside(step):
        number = mine + step + nb
        at = (slab + total + number // nb - 1) % total
        return device(place_of(number % nb, at), at)

    after, before = beside(1), beside(-1)

    moves = (
        (p_hbm, p_ref),
        (f_hbm, f_ref),
        (desc_hbm, desc),
        (perm_hbm, perm_ref),
        (mass_hbm, mass_ref),
        (w_high_hbm, w_high),
        (w_low_hbm, w_low),
        (list_hbm, lists),
        (one_hbm, one),
        (two_hbm, two_ref),
        (three_hbm, three_ref),
        (out_w_hbm, out_w_ref),
        (s_high_hbm, s_high),
        (s_low_hbm, s_low),
    )
    loads = [
        pltpu.make_async_copy(source, dest, local_sem.at[at])
        for at, (source, dest) in enumerate(moves)
    ]
    for load in loads:
        load.start()

    barrier = pltpu.get_barrier_semaphore()

    def greet(off, carry):
        pl.semaphore_signal(
            barrier, inc=1, device_id=device((me + off) % nb, slab), device_id_type=MESH
        )
        return carry

    lax.fori_loop(1, nb, greet, 0)
    for other in (device(me, up), device(me, down), before, after):
        pl.semaphore_signal(barrier, inc=1, device_id=other, device_id_type=MESH)
    for load in loads[:2]:
        load.wait()
    kick_buf[...] = p_ref[...] + 0.5 * TIME_STEP * f_ref[...]
    pl.semaphore_wait(barrier, nb - 1 + 4)

    def lanes_of(place):
        return pl.ds(pl.multiple_of(block_of(place) * block, LANE), block)

    sources = (q_hbm, n_hbm, kick_buf)

    def send_in(which, dest, source):
        return pltpu.make_async_remote_copy(
            src_ref=sources[which].at[:, :, lanes_of(dest)],
            dst_ref=recv_in.at[which, source],
            send_sem=in_send.at[which, dest],
            recv_sem=in_recv.at[which, source],
            device_id=device(dest, slab),
            device_id_type=MESH,
        )

    def start_in(off, carry):
        for which in range(3):
            send_in(which, (me + off) % nb, me).start()
        return carry

    lax.fori_loop(1, nb, start_in, 0)
    owns = [
        pltpu.make_async_copy(
            sources[which].at[:, :, lanes_of(me)], recv_in.at[which, me], own_sem.at[which]
        )
        for which in range(3)
    ]
    for own in owns:
        own.start()

    for load in loads[2:]:
        load.wait()
    desc_p[...] = dot32(desc[...], perm_ref[...]).astype(jnp.bfloat16)
    two_t[...] = jnp.transpose(two_ref[...])
    three_t[...] = jnp.transpose(three_ref[...])

    for own in owns:
        own.wait()

    def wait_in(off, carry):
        for which in range(3):
            send_in(which, (me + off) % nb, (me + off) % nb).wait_recv()
        return carry

    lax.fori_loop(1, nb, wait_in, 0)

    for which, part in ((0, 0), (2, 1), (1, 2)):
        for place in range(nb):
            for comp in range(3):
                row = part * beads + place * bl
                xs[row : row + bl, comp * block : (comp + 1) * block] = recv_in[which, place, comp]
    heavy = jnp.concatenate(
        [mass_ref[pl.ds(mine * wide + h, 1), :] for h in range(wide)] * 3, axis=1
    )
    x_all = jnp.concatenate(
        [
            xs[0:beads, :],
            xs[beads : 2 * beads, :] / heavy,
            xs[2 * beads : 3 * beads, :] / jnp.sqrt(heavy),
        ],
        axis=0,
    )
    y_all = table_dot(w_high[...], w_low[...], x_all)
    contracted = y_all[2 * beads : 2 * beads + nc]
    for comp in range(3):
        for cb in range(nc):
            ext[comp, cb, :, LANE : LANE + block] = contracted[
                cb : cb + 1, comp * block : (comp + 1) * block
            ]
    y_new = y_all[0:beads]
    y_mom = y_all[beads : 2 * beads] * heavy
    for arr, value in ((0, y_new), (1, y_mom)):
        for place in range(nb):
            for comp in range(3):
                y_buf[arr, place, comp] = value[
                    place * bl : (place + 1) * bl, comp * block : (comp + 1) * block
                ]

    far = LANE + block
    halos = [
        pltpu.make_async_remote_copy(
            src_ref=ext.at[:, :, :, pl.ds(block, LANE)],
            dst_ref=ext.at[:, :, :, pl.ds(0, LANE)],
            send_sem=halo_send.at[0],
            recv_sem=halo_recv.at[0],
            device_id=after,
            device_id_type=MESH,
        ),
        pltpu.make_async_remote_copy(
            src_ref=ext.at[:, :, :, pl.ds(LANE, LANE)],
            dst_ref=ext.at[:, :, :, pl.ds(far, LANE)],
            send_sem=halo_send.at[1],
            recv_sem=halo_recv.at[1],
            device_id=before,
            device_id_type=MESH,
        ),
    ]
    for halo in halos:
        halo.start()

    def back_lanes(source):
        return pl.ds(pl.multiple_of(LANE + block_of(source) * block, LANE), block)

    def send_y(arr, dest, source):
        return pltpu.make_async_remote_copy(
            src_ref=y_buf.at[arr, dest],
            dst_ref=back.at[arr, :, :, back_lanes(source)],
            send_sem=y_send.at[arr, dest],
            recv_sem=y_recv.at[arr, source],
            device_id=device(dest, slab),
            device_id_type=MESH,
        )

    for arr in range(2):

        def start_y(off, carry, arr=arr):
            send_y(arr, (me + off) % nb, me).start()
            return carry

        lax.fori_loop(1, nb, start_y, 0)
    y_own = [
        pltpu.make_async_copy(
            y_buf.at[arr, me], back.at[arr, :, :, back_lanes(me)], own_sem.at[arr]
        )
        for arr in range(2)
    ]
    for own in y_own:
        own.start()
    for halo in halos:
        halo.wait_recv()

    width = lists.shape[0]
    for h in range(wide):
        for pair in range(width // 16):
            picks = [tile_lists(lists, mine * wide + h, 2 * pair + k) for k in range(2)]
            for cb in range(nc):
                halves = []
                for low, first, third in picks:
                    apart = []
                    for comp in range(3):
                        rows = [
                            ext[comp, cb, :, (h + k) * LANE : (h + k + 1) * LANE]
                            for k in range(3)
                        ]
                        apart.append(gather_near(rows, low, first, third))
                    halves.append(apart + [closeness(apart, 1.0)])
                for entry in range(4):
                    at = entry * width + 16 * pair
                    env_buf[
                        cb // 2,
                        at : at + 16,
                        ((cb % 2) * wide + h) * LANE : ((cb % 2) * wide + h + 1) * LANE,
                    ] = (
                        jnp.concatenate([halves[0][entry], halves[1][entry]], axis=0).astype(
                            jnp.bfloat16
                        )
                    )
    chunk = 512
    depth = one.shape[1]

    def two_contracted(step, carry):
        env = env_buf[step]
        total_one = None
        for low_at in range(0, depth, chunk):
            high_at = min(low_at + chunk, depth)
            piece = jnp.tanh(dot32(desc_p[low_at:high_at, :], env)).astype(jnp.bfloat16)
            term = dot32(one[:, low_at:high_at], piece)
            total_one = term if total_one is None else total_one + term
        layer = jnp.tanh(total_one).astype(jnp.bfloat16)
        for matrix in (two_t, three_t):
            layer = jnp.tanh(dot32(matrix[...], layer)).astype(jnp.bfloat16)
        neural[step] = dot32(out_w_ref[...], layer)
        return carry

    lax.fori_loop(0, nc // 2, two_contracted, 0)

    for comp in range(3):
        rows = jnp.concatenate([
                neural[cb // 2, comp : comp + 1, (cb % 2) * block : (cb % 2 + 1) * block]
                for cb in range(nc)
            ], axis=0)
        spread = table_dot(s_high[...], s_low[...], rows)
        for place in range(nb):
            s_buf[place, comp] = spread[place * bl : (place + 1) * bl, :]

    def send_s(dest, source):
        return pltpu.make_async_remote_copy(
            src_ref=s_buf.at[dest],
            dst_ref=s_recv.at[:, :, lanes_of(source)],
            send_sem=s_send.at[dest],
            recv_sem=s_recv_sem.at[source],
            device_id=device(dest, slab),
            device_id_type=MESH,
        )

    def start_s(off, carry):
        send_s((me + off) % nb, me).start()
        return carry

    lax.fori_loop(1, nb, start_s, 0)
    s_own = pltpu.make_async_copy(s_buf.at[me], s_recv.at[:, :, lanes_of(me)], own_sem.at[2])
    s_own.start()

    for own in y_own:
        own.wait()
    for arr in range(2):

        def wait_y(off, carry, arr=arr):
            send_y(arr, (me + off) % nb, (me + off) % nb).wait_recv()
            return carry

        lax.fori_loop(1, nb, wait_y, 0)

    edges = [
        pltpu.make_async_remote_copy(
            src_ref=back.at[0, :, :, pl.ds(last, LANE)],
            dst_ref=back.at[0, :, :, pl.ds(0, LANE)],
            send_sem=edge_send.at[0],
            recv_sem=edge_recv.at[0],
            device_id=device(me, up),
            device_id_type=MESH,
        ),
        pltpu.make_async_remote_copy(
            src_ref=back.at[0, :, :, pl.ds(LANE, LANE)],
            dst_ref=back.at[0, :, :, pl.ds(last + LANE, LANE)],
            send_sem=edge_send.at[1],
            recv_sem=edge_recv.at[1],
            device_id=device(me, down),
            device_id_type=MESH,
        ),
    ]
    for edge in edges:
        edge.start()

    def one_tile(tile, carry):
        at = [pl.ds(pl.multiple_of((tile + k) * LANE, LANE), LANE) for k in range(3)]
        sums = [[None] * bl for _ in range(3)]
        for group in range(width // 8):
            low, first, third = tile_lists(lists, tile, group)
            for bead in range(bl):
                apart = []
                for comp in range(3):
                    rows = [back[0, comp, bead : bead + 1, at[k]] for k in range(3)]
                    apart.append(gather_near(rows, low, first, third))
                close = closeness(apart, PAIR_STRENGTH)
                for comp in range(3):
                    term = apart[comp] * close
                    old = sums[comp][bead]
                    sums[comp][bead] = term if old is None else old + term
        for comp in range(3):
            pair_buf[comp, :, at[0]] = jnp.concatenate(
                [jnp.sum(part, axis=0, keepdims=True) for part in sums[comp]], axis=0
            )
        return carry

    def inner_tiles(step, carry):
        for k in range(2):
            one_tile(1 + 2 * step + k, carry)
        return carry

    lax.fori_loop(0, (tiles - 2) // 2, inner_tiles, 0)
    for edge in edges:
        edge.wait_recv()

    def outer_tile(which, carry):
        return one_tile(which * (tiles - 1), carry)

    lax.fori_loop(0, 2, outer_tile, 0)

    s_own.wait()

    def wait_s(off, carry):
        send_s((me + off) % nb, (me + off) % nb).wait_recv()
        return carry

    lax.fori_loop(1, nb, wait_s, 0)
    force = pair_buf[...] + s_recv[...]
    out_f[...] = force
    out_m[...] = back[1, :, :, LANE : LANE + last] + 0.5 * TIME_STEP * force
    out_q[...] = back[0, :, :, LANE : LANE + last]

    def drain(off, carry):
        dest = (me + off) % nb
        for which in range(3):
            send_in(which, dest, me).wait_send()
        for arr in range(2):
            send_y(arr, dest, me).wait_send()
        send_s(dest, me).wait_send()
        return carry

    lax.fori_loop(1, nb, drain, 0)
    for copy in halos + edges:
        copy.wait_send()


def body(
    positions,
    momenta,
    force_old,
    noise,
    mass,
    pair_list,
    desc_w,
    hidden_one,
    hidden_two,
    hidden_three,
    out_w,
):
    nb = lax.axis_size("bead")
    bl, _, atoms = positions.shape
    beads = nb * bl
    block = atoms // nb
    width = pair_list.shape[1]
    env, wide = desc_w.shape
    hid = hidden_one.shape[1]
    table, contract = step_tables(beads, NC)
    w_high, w_low = split_table(table)
    s_high, s_low = split_table(contract.T * (beads / NC))
    perm = np.zeros((env, env), np.float32)
    for j in range(width):
        for entry in range(4):
            perm[4 * j + entry, entry * width + j] = 1.0
    perm = jnp.asarray(perm, jnp.bfloat16)

    def flip(x):
        return jnp.transpose(x, (1, 0, 2))

    out = jax.ShapeDtypeStruct((3, bl, atoms), jnp.float32)
    f32, bf16 = jnp.float32, jnp.bfloat16
    dma = pltpu.SemaphoreType.DMA
    new_q, new_m, new_f = pl.pallas_call(
        functools.partial(kernel, nb),
        out_shape=(out, out, out),
        in_specs=[pl.BlockSpec(memory_space=pltpu.HBM)] * 16,
        out_specs=(pl.BlockSpec(memory_space=pltpu.VMEM),) * 3,
        scratch_shapes=[
            pltpu.VMEM((3, bl, atoms), f32),
            pltpu.VMEM((3, bl, atoms), f32),
            pltpu.VMEM((atoms // LANE, LANE), f32),
            pltpu.VMEM((hid, hid), bf16),
            pltpu.VMEM((hid, hid), bf16),
            pltpu.VMEM((3, hid), bf16),
            pltpu.VMEM((env, env), bf16),
            pltpu.VMEM(w_high.shape, bf16),
            pltpu.VMEM(w_low.shape, bf16),
            pltpu.VMEM(s_high.shape, bf16),
            pltpu.VMEM(s_low.shape, bf16),
            pltpu.VMEM((3, bl, atoms), f32),
            pltpu.VMEM((3, nb, 3, bl, block), f32),
            pltpu.VMEM((3 * beads, 3 * block), f32),
            pltpu.VMEM((2, nb, 3, bl, block), f32),
            pltpu.VMEM((2, 3, bl, atoms + 2 * LANE), f32),
            pltpu.VMEM((3, NC, 1, block + 2 * LANE), f32),
            pltpu.VMEM((NC // 2, 3, 2 * block), f32),
            pltpu.VMEM((nb, 3, bl, block), f32),
            pltpu.VMEM((3, bl, atoms), f32),
            pltpu.VMEM((3, bl, atoms), f32),
            pltpu.VMEM((width, atoms), jnp.int32),
            pltpu.VMEM((wide, env), bf16),
            pltpu.VMEM((wide, env), bf16),
            pltpu.VMEM((hid, wide), bf16),
            pltpu.VMEM((hid, hid), bf16),
            pltpu.VMEM((hid, hid), bf16),
            pltpu.VMEM((NC // 2, env, 2 * block), bf16),
            dma((14,)),
            dma((3,)),
            dma((3, nb)),
            dma((3, nb)),
            dma((2, nb)),
            dma((2, nb)),
            dma((nb,)),
            dma((nb,)),
            dma((2,)),
            dma((2,)),
            dma((2,)),
            dma((2,)),
        ],
        compiler_params=pltpu.CompilerParams(
            collective_id=0, has_side_effects=True, vmem_limit_bytes=66519040
        ),
    )(
        flip(positions),
        flip(noise),
        flip(momenta),
        flip(force_old),
        mass.reshape(atoms // LANE, LANE),
        pair_list.T,
        desc_w.T,
        hidden_one.T,
        hidden_two,
        hidden_three,
        out_w.T,
        perm,
        w_high,
        w_low,
        s_high,
        s_low,
    )
    return flip(new_q), flip(new_m), flip(new_f)


def solution(mesh):
    whole = P("bead", None, ("slab", "grp"))
    placed = (whole,) * 4 + (P(("slab", "grp")), P(("slab", "grp"), None)) + (P(),) * 5
    return jax.shard_map(
        body, mesh=mesh, in_specs=placed, out_specs=(whole,) * 3, check_vma=False
    )
```

```python
import functools

import jax
import jax.numpy as jnp
import numpy as np
from jax import lax
from jax.experimental import pallas as pl
from jax.experimental.pallas import tpu as pltpu
from jax.sharding import PartitionSpec as P

BEADS = 64
NC = 8
LANE = 128
TIME_STEP = 0.1
CYCLE_FREQ = 5.0
CENTROID_FRICTION = 1.0
PAIR_STRENGTH = 0.5
MESH = pl.DeviceIdType.MESH


def cycle_tables(beads, contracted):
    index = np.arange(beads, dtype=np.float64)
    mode = np.arange(beads)[None, :]
    angle = 2.0 * np.pi * index[:, None] * index[None, :] / beads
    half = beads // 2
    root_one = 1.0 / np.sqrt(beads)
    root_two = np.sqrt(2.0 / beads)
    alternate = np.where(np.arange(beads) % 2 == 0, 1.0, -1.0)[:, None]
    basis = np.where(
        mode == 0,
        root_one,
        np.where(
            mode < half,
            root_two * np.cos(angle),
            np.where(mode == half, root_one * alternate, root_two * np.sin(angle)),
        ),
    )
    freq = 2.0 * CYCLE_FREQ * np.sin(np.pi * index / beads)
    spacing = index[None, :] / beads - np.arange(contracted)[:, None] / contracted
    kernel = np.ones_like(spacing)
    for order in range(1, contracted // 2):
        kernel = kernel + 2.0 * np.cos(2.0 * np.pi * order * spacing)
    kernel = kernel + np.cos(np.pi * contracted * spacing)
    return basis, freq, kernel / beads


def step_tables(beads, contracted):
    basis, freq, contract = cycle_tables(beads, contracted)
    step = 0.5 * TIME_STEP
    moving = freq > 0.0
    safe = np.where(moving, freq, 1.0)
    cos = np.where(moving, np.cos(safe * step), 1.0)
    sin_over = np.where(moving, np.sin(safe * step) / safe, step)
    sin_times = np.where(moving, np.sin(safe * step) * safe, 0.0)
    keep = np.exp(-np.where(moving, 2.0 * freq, CENTROID_FRICTION) * TIME_STEP)
    kick = np.sqrt(1.0 - keep * keep)

    def both(diag):
        return (basis * diag[None, :]) @ basis.T

    q_rows = np.concatenate(
        [
            both(cos * cos - keep * sin_over * sin_times),
            both(cos * sin_over * (1.0 + keep)),
            basis * (sin_over * kick)[None, :],
        ],
        axis=1,
    )
    p_rows = np.concatenate(
        [
            both(-cos * sin_times * (1.0 + keep)),
            both(cos * cos * keep - sin_over * sin_times),
            basis * (cos * kick)[None, :],
        ],
        axis=1,
    )
    return np.concatenate([q_rows, p_rows, contract @ q_rows], axis=0), contract


def split_table(table):
    table = jnp.asarray(table.astype(np.float32))
    high = table.astype(jnp.bfloat16)
    low = (table - high.astype(jnp.float32)).astype(jnp.bfloat16)
    return high, low


def dot32(left, right):
    return jnp.dot(left, right, preferred_element_type=jnp.float32)


def table_dot(high, low, x):
    x_high = x.astype(jnp.bfloat16)
    x_low = (x - x_high.astype(jnp.float32)).astype(jnp.bfloat16)
    return dot32(high, x_high) + (dot32(high, x_low) + dot32(low, x_high))


def gather_near(rows, low, first, third):
    got = [
        jnp.take_along_axis(
            jnp.broadcast_to(row, low.shape), low, axis=1, mode="promise_in_bounds"
        )
        for row in rows
    ]
    return jnp.where(first, got[0], jnp.where(third, got[2], got[1])) - rows[1]


def tile_lists(list_ref, tile, group):
    lanes = pl.ds(pl.multiple_of(tile * LANE, LANE), LANE)
    index = list_ref[8 * group : 8 * group + 8, lanes] - tile * LANE
    return index & (LANE - 1), index < LANE, index >= 2 * LANE


def closeness(apart, scale):
    return scale / (1.0 + (apart[0] * apart[0] + apart[1] * apart[1] + apart[2] * apart[2]))


def kernel(
    groups,
    q_hbm,
    n_hbm,
    p_hbm,
    f_hbm,
    mass_hbm,
    list_hbm,
    desc_hbm,
    one_hbm,
    two_hbm,
    three_hbm,
    out_w_hbm,
    perm_hbm,
    w_high_hbm,
    w_low_hbm,
    s_high_hbm,
    s_low_hbm,
    out_q,
    out_m,
    out_f,
    p_ref,
    f_ref,
    mass_ref,
    two_ref,
    three_ref,
    out_w_ref,
    perm_ref,
    w_high,
    w_low,
    s_high,
    s_low,
    sent,
    recv_in,
    xs,
    y_buf,
    back,
    ext,
    neural,
    s_buf,
    s_recv,
    pair_buf,
    lists,
    desc,
    desc_p,
    one,
    two_t,
    three_t,
    env_buf,
    layer_buf,
    local_sem,
    own_sem,
    in_send,
    in_recv,
    y_send,
    y_recv,
    s_send,
    s_recv_sem,
    halo_send,
    halo_recv,
    edge_send,
    edge_recv,
):
    nb = groups
    bl = p_ref.shape[1]
    last = p_ref.shape[2]
    block = p_ref.shape[2] // nb
    tiles = p_ref.shape[2] // LANE
    wide = block // LANE
    beads = nb * bl
    nc = ext.shape[1]
    me = lax.axis_index("bead")
    slabs, cores = lax.axis_size("slab"), lax.axis_size("grp")
    total = slabs * cores
    slab = lax.axis_index("slab") * cores + lax.axis_index("grp")

    def device(place, at):
        return {"bead": place, "slab": at // cores, "grp": at % cores}

    up, down = (slab + 1) % total, (slab + total - 1) % total

    def block_of(place, at=slab):
        if nb != 16:
            return place
        core, shift = at % cores, (3 * (at // cores)) % 4
        x, z = (place // 4 + 4 - shift) % 4, place % 4
        along_x = 4 * z + x + (z % 2) * (3 - 2 * x)
        along_z = 4 * x + 3 - z + (x % 2) * (2 * z - 3)
        return along_x + core * (along_z - along_x)

    def place_of(number, at):
        if nb != 16:
            return number
        core, shift = at % cores, (3 * (at // cores)) % 4
        far, near = number // 4, number % 4
        x_first = 4 * ((near + (far % 2) * (3 - 2 * near) + shift) % 4) + far
        z_first = 4 * ((far + shift) % 4) + 3 - near + (far % 2) * (2 * near - 3)
        return x_first + core * (z_first - x_first)

    mine = block_of(me)

    def beside(step):
        number = mine + step + nb
        at = (slab + total + number // nb - 1) % total
        return device(place_of(number % nb, at), at)

    after, before = beside(1), beside(-1)

    moves = (
        (p_hbm, p_ref),
        (f_hbm, f_ref),
        (q_hbm, sent.at[0]),
        (n_hbm, sent.at[2]),
        (desc_hbm, desc),
        (perm_hbm, perm_ref),
        (mass_hbm, mass_ref),
        (w_high_hbm, w_high),
        (w_low_hbm, w_low),
        (list_hbm, lists),
        (one_hbm, one),
        (two_hbm, two_ref),
        (three_hbm, three_ref),
        (out_w_hbm, out_w_ref),
        (s_high_hbm, s_high),
        (s_low_hbm, s_low),
    )
    loads = [
        pltpu.make_async_copy(source, dest, local_sem.at[at])
        for at, (source, dest) in enumerate(moves)
    ]
    for load in loads:
        load.start()

    barrier = pltpu.get_barrier_semaphore()

    def greet(off, carry):
        pl.semaphore_signal(
            barrier, inc=1, device_id=device((me + off) % nb, slab), device_id_type=MESH
        )
        return carry

    lax.fori_loop(1, nb, greet, 0)
    for other in (device(me, up), device(me, down), before, after):
        pl.semaphore_signal(barrier, inc=1, device_id=other, device_id_type=MESH)
    for load in loads[:4]:
        load.wait()
    sent[1] = p_ref[...] + 0.5 * TIME_STEP * f_ref[...]
    pl.semaphore_wait(barrier, nb - 1 + 4)

    def lanes_of(place):
        return pl.ds(pl.multiple_of(block_of(place) * block, LANE), block)

    def send_in(dest, source):
        return pltpu.make_async_remote_copy(
            src_ref=sent.at[:, :, :, lanes_of(dest)],
            dst_ref=recv_in.at[source],
            send_sem=in_send.at[dest],
            recv_sem=in_recv.at[source],
            device_id=device(dest, slab),
            device_id_type=MESH,
        )

    def start_in(off, carry):
        send_in((me + off) % nb, me).start()
        return carry

    lax.fori_loop(1, nb, start_in, 0)
    own_in = pltpu.make_async_copy(sent.at[:, :, :, lanes_of(me)], recv_in.at[me], own_sem.at[0])
    own_in.start()

    for load in loads[4:]:
        load.wait()
    desc_p[...] = dot32(desc[...], perm_ref[...]).astype(jnp.bfloat16)
    two_t[...] = jnp.transpose(two_ref[...])
    three_t[...] = jnp.transpose(three_ref[...])

    own_in.wait()

    def wait_in(off, carry):
        send_in((me + off) % nb, (me + off) % nb).wait_recv()
        return carry

    lax.fori_loop(1, nb, wait_in, 0)

    for part in range(3):
        for place in range(nb):
            for comp in range(3):
                row = part * beads + place * bl
                xs[row : row + bl, comp * block : (comp + 1) * block] = recv_in[place, part, comp]
    heavy = jnp.concatenate(
        [mass_ref[pl.ds(mine * wide + h, 1), :] for h in range(wide)] * 3, axis=1
    )
    x_all = jnp.concatenate(
        [
            xs[0:beads, :],
            xs[beads : 2 * beads, :] / heavy,
            xs[2 * beads : 3 * beads, :] / jnp.sqrt(heavy),
        ],
        axis=0,
    )
    y_all = table_dot(w_high[...], w_low[...], x_all)
    contracted = y_all[2 * beads : 2 * beads + nc]
    for comp in range(3):
        for cb in range(nc):
            ext[comp, cb, :, LANE : LANE + block] = contracted[
                cb : cb + 1, comp * block : (comp + 1) * block
            ]
    y_new = y_all[0:beads]
    y_mom = y_all[beads : 2 * beads] * heavy
    for arr, value in ((0, y_new), (1, y_mom)):
        for place in range(nb):
            for comp in range(3):
                y_buf[place, arr, comp] = value[
                    place * bl : (place + 1) * bl, comp * block : (comp + 1) * block
                ]

    far = LANE + block
    halos = [
        pltpu.make_async_remote_copy(
            src_ref=ext.at[:, :, :, pl.ds(block, LANE)],
            dst_ref=ext.at[:, :, :, pl.ds(0, LANE)],
            send_sem=halo_send.at[0],
            recv_sem=halo_recv.at[0],
            device_id=after,
            device_id_type=MESH,
        ),
        pltpu.make_async_remote_copy(
            src_ref=ext.at[:, :, :, pl.ds(LANE, LANE)],
            dst_ref=ext.at[:, :, :, pl.ds(far, LANE)],
            send_sem=halo_send.at[1],
            recv_sem=halo_recv.at[1],
            device_id=before,
            device_id_type=MESH,
        ),
    ]
    for halo in halos:
        halo.start()

    def back_lanes(source):
        return pl.ds(pl.multiple_of(LANE + block_of(source) * block, LANE), block)

    def send_y(dest, source):
        return pltpu.make_async_remote_copy(
            src_ref=y_buf.at[dest],
            dst_ref=back.at[:, :, :, back_lanes(source)],
            send_sem=y_send.at[dest],
            recv_sem=y_recv.at[source],
            device_id=device(dest, slab),
            device_id_type=MESH,
        )

    def start_y(off, carry):
        send_y((me + off) % nb, me).start()
        return carry

    lax.fori_loop(1, nb, start_y, 0)
    y_own = pltpu.make_async_copy(y_buf.at[me], back.at[:, :, :, back_lanes(me)], own_sem.at[1])
    y_own.start()
    for halo in halos:
        halo.wait_recv()

    width = lists.shape[0]
    for h in range(wide):
        for pair in range(width // 16):
            picks = [tile_lists(lists, mine * wide + h, 2 * pair + k) for k in range(2)]
            for cb in range(nc):
                halves = []
                for low, first, third in picks:
                    apart = []
                    for comp in range(3):
                        rows = [
                            ext[comp, cb, :, (h + k) * LANE : (h + k + 1) * LANE]
                            for k in range(3)
                        ]
                        apart.append(gather_near(rows, low, first, third))
                    halves.append(apart + [closeness(apart, 1.0)])
                for entry in range(4):
                    at = entry * width + 16 * pair
                    env_buf[
                        cb // 2,
                        at : at + 16,
                        ((cb % 2) * wide + h) * LANE : ((cb % 2) * wide + h + 1) * LANE,
                    ] = (
                        jnp.concatenate([halves[0][entry], halves[1][entry]], axis=0).astype(
                            jnp.bfloat16
                        )
                    )
    chunk = 512
    depth = one.shape[1]

    def two_contracted(step, carry):
        env = env_buf[step]
        total_one = None
        for low_at in range(0, depth, chunk):
            high_at = min(low_at + chunk, depth)
            piece = jnp.tanh(dot32(desc_p[low_at:high_at, :], env)).astype(jnp.bfloat16)
            term = dot32(one[:, low_at:high_at], piece)
            total_one = term if total_one is None else total_one + term
        layer_buf[step] = jnp.tanh(total_one).astype(jnp.bfloat16)
        return carry

    lax.fori_loop(0, nc // 2, two_contracted, 0)
    layers = [layer_buf[step] for step in range(nc // 2)]
    for matrix in (two_t, three_t):
        layers = [jnp.tanh(dot32(matrix[...], layer)).astype(jnp.bfloat16) for layer in layers]
    for step, layer in enumerate(layers):
        neural[step] = dot32(out_w_ref[...], layer)

    for comp in range(3):
        rows = jnp.concatenate([
                neural[cb // 2, comp : comp + 1, (cb % 2) * block : (cb % 2 + 1) * block]
                for cb in range(nc)
            ], axis=0)
        spread = table_dot(s_high[...], s_low[...], rows)
        for place in range(nb):
            s_buf[place, comp] = spread[place * bl : (place + 1) * bl, :]

    def send_s(dest, source):
        return pltpu.make_async_remote_copy(
            src_ref=s_buf.at[dest],
            dst_ref=s_recv.at[:, :, lanes_of(source)],
            send_sem=s_send.at[dest],
            recv_sem=s_recv_sem.at[source],
            device_id=device(dest, slab),
            device_id_type=MESH,
        )

    def start_s(off, carry):
        send_s((me + off) % nb, me).start()
        return carry

    lax.fori_loop(1, nb, start_s, 0)
    s_own = pltpu.make_async_copy(s_buf.at[me], s_recv.at[:, :, lanes_of(me)], own_sem.at[2])
    s_own.start()

    y_own.wait()

    def wait_y(off, carry):
        send_y((me + off) % nb, (me + off) % nb).wait_recv()
        return carry

    lax.fori_loop(1, nb, wait_y, 0)

    edges = [
        pltpu.make_async_remote_copy(
            src_ref=back.at[0, :, :, pl.ds(last, LANE)],
            dst_ref=back.at[0, :, :, pl.ds(0, LANE)],
            send_sem=edge_send.at[0],
            recv_sem=edge_recv.at[0],
            device_id=device(me, up),
            device_id_type=MESH,
        ),
        pltpu.make_async_remote_copy(
            src_ref=back.at[0, :, :, pl.ds(LANE, LANE)],
            dst_ref=back.at[0, :, :, pl.ds(last + LANE, LANE)],
            send_sem=edge_send.at[1],
            recv_sem=edge_recv.at[1],
            device_id=device(me, down),
            device_id_type=MESH,
        ),
    ]
    for edge in edges:
        edge.start()

    def one_tile(tile, carry):
        at = [pl.ds(pl.multiple_of((tile + k) * LANE, LANE), LANE) for k in range(3)]
        sums = [[None] * bl for _ in range(3)]
        for group in range(width // 8):
            low, first, third = tile_lists(lists, tile, group)
            for bead in range(bl):
                apart = []
                for comp in range(3):
                    rows = [back[0, comp, bead : bead + 1, at[k]] for k in range(3)]
                    apart.append(gather_near(rows, low, first, third))
                close = closeness(apart, PAIR_STRENGTH)
                for comp in range(3):
                    term = apart[comp] * close
                    old = sums[comp][bead]
                    sums[comp][bead] = term if old is None else old + term
        for comp in range(3):
            pair_buf[comp, :, at[0]] = jnp.concatenate(
                [jnp.sum(part, axis=0, keepdims=True) for part in sums[comp]], axis=0
            )
        return carry

    together = next(n for n in (5, 3, 2, 1) if (tiles - 2) % n == 0)

    def inner_tiles(step, carry):
        for k in range(together):
            one_tile(1 + together * step + k, carry)
        return carry

    lax.fori_loop(0, (tiles - 2) // together, inner_tiles, 0)
    for edge in edges:
        edge.wait_recv()

    def outer_tile(which, carry):
        return one_tile(which * (tiles - 1), carry)

    lax.fori_loop(0, 2, outer_tile, 0)

    s_own.wait()

    def wait_s(off, carry):
        send_s((me + off) % nb, (me + off) % nb).wait_recv()
        return carry

    lax.fori_loop(1, nb, wait_s, 0)
    force = pair_buf[...] + s_recv[...]
    out_f[...] = force
    out_m[...] = back[1, :, :, LANE : LANE + last] + 0.5 * TIME_STEP * force
    out_q[...] = back[0, :, :, LANE : LANE + last]

    def drain(off, carry):
        dest = (me + off) % nb
        send_in(dest, me).wait_send()
        send_y(dest, me).wait_send()
        send_s(dest, me).wait_send()
        return carry

    lax.fori_loop(1, nb, drain, 0)
    for copy in halos + edges:
        copy.wait_send()


def body(
    positions,
    momenta,
    force_old,
    noise,
    mass,
    pair_list,
    desc_w,
    hidden_one,
    hidden_two,
    hidden_three,
    out_w,
):
    nb = lax.axis_size("bead")
    bl, _, atoms = positions.shape
    beads = nb * bl
    block = atoms // nb
    width = pair_list.shape[1]
    env, wide = desc_w.shape
    hid = hidden_one.shape[1]
    table, contract = step_tables(beads, NC)
    w_high, w_low = split_table(table)
    s_high, s_low = split_table(contract.T * (beads / NC))
    perm = np.zeros((env, env), np.float32)
    for j in range(width):
        for entry in range(4):
            perm[4 * j + entry, entry * width + j] = 1.0
    perm = jnp.asarray(perm, jnp.bfloat16)

    def flip(x):
        return jnp.transpose(x, (1, 0, 2))

    out = jax.ShapeDtypeStruct((3, bl, atoms), jnp.float32)
    f32, bf16 = jnp.float32, jnp.bfloat16
    dma = pltpu.SemaphoreType.DMA
    new_q, new_m, new_f = pl.pallas_call(
        functools.partial(kernel, nb),
        out_shape=(out, out, out),
        in_specs=[pl.BlockSpec(memory_space=pltpu.HBM)] * 16,
        out_specs=(pl.BlockSpec(memory_space=pltpu.VMEM),) * 3,
        scratch_shapes=[
            pltpu.VMEM((3, bl, atoms), f32),
            pltpu.VMEM((3, bl, atoms), f32),
            pltpu.VMEM((atoms // LANE, LANE), f32),
            pltpu.VMEM((hid, hid), bf16),
            pltpu.VMEM((hid, hid), bf16),
            pltpu.VMEM((3, hid), bf16),
            pltpu.VMEM((env, env), bf16),
            pltpu.VMEM(w_high.shape, bf16),
            pltpu.VMEM(w_low.shape, bf16),
            pltpu.VMEM(s_high.shape, bf16),
            pltpu.VMEM(s_low.shape, bf16),
            pltpu.VMEM((3, 3, bl, atoms), f32),
            pltpu.VMEM((nb, 3, 3, bl, block), f32),
            pltpu.VMEM((3 * beads, 3 * block), f32),
            pltpu.VMEM((nb, 2, 3, bl, block), f32),
            pltpu.VMEM((2, 3, bl, atoms + 2 * LANE), f32),
            pltpu.VMEM((3, NC, 1, block + 2 * LANE), f32),
            pltpu.VMEM((NC // 2, 3, 2 * block), f32),
            pltpu.VMEM((nb, 3, bl, block), f32),
            pltpu.VMEM((3, bl, atoms), f32),
            pltpu.VMEM((3, bl, atoms), f32),
            pltpu.VMEM((width, atoms), jnp.int32),
            pltpu.VMEM((wide, env), bf16),
            pltpu.VMEM((wide, env), bf16),
            pltpu.VMEM((hid, wide), bf16),
            pltpu.VMEM((hid, hid), bf16),
            pltpu.VMEM((hid, hid), bf16),
            pltpu.VMEM((NC // 2, env, 2 * block), bf16),
            pltpu.VMEM((NC // 2, hid, 2 * block), bf16),
            dma((16,)),
            dma((3,)),
            dma((nb,)),
            dma((nb,)),
            dma((nb,)),
            dma((nb,)),
            dma((nb,)),
            dma((nb,)),
            dma((2,)),
            dma((2,)),
            dma((2,)),
            dma((2,)),
        ],
        compiler_params=pltpu.CompilerParams(
            collective_id=0, has_side_effects=True, vmem_limit_bytes=50331648
        ),
    )(*[pltpu.with_memory_space_constraint(x, pltpu.HBM) for x in (

        flip(positions),
        flip(noise),
        flip(momenta),
        flip(force_old),
        mass.reshape(atoms // LANE, LANE),
        pair_list.T,
        desc_w.T,
        hidden_one.T,
        hidden_two,
        hidden_three,
        out_w.T,
        perm,
        w_high,
        w_low,
        s_high,
        s_low,
        )])
    return flip(new_q), flip(new_m), flip(new_f)


def solution(mesh):
    whole = P("bead", None, ("slab", "grp"))
    placed = (whole,) * 4 + (P(("slab", "grp")), P(("slab", "grp"), None)) + (P(),) * 5
    return jax.shard_map(
        body, mesh=mesh, in_specs=placed, out_specs=(whole,) * 3, check_vma=False
    )
```

```python
import functools

import jax
import jax.numpy as jnp
import numpy as np
from jax import lax
from jax.experimental import pallas as pl
from jax.experimental.pallas import tpu as pltpu
from jax.sharding import PartitionSpec as P

BEADS = 64
NC = 8
LANE = 128
TIME_STEP = 0.1
CYCLE_FREQ = 5.0
CENTROID_FRICTION = 1.0
PAIR_STRENGTH = 0.5
MESH = pl.DeviceIdType.MESH


def cycle_tables(beads, contracted):
    index = np.arange(beads, dtype=np.float64)
    mode = np.arange(beads)[None, :]
    angle = 2.0 * np.pi * index[:, None] * index[None, :] / beads
    half = beads // 2
    root_one = 1.0 / np.sqrt(beads)
    root_two = np.sqrt(2.0 / beads)
    alternate = np.where(np.arange(beads) % 2 == 0, 1.0, -1.0)[:, None]
    basis = np.where(
        mode == 0,
        root_one,
        np.where(
            mode < half,
            root_two * np.cos(angle),
            np.where(mode == half, root_one * alternate, root_two * np.sin(angle)),
        ),
    )
    freq = 2.0 * CYCLE_FREQ * np.sin(np.pi * index / beads)
    spacing = index[None, :] / beads - np.arange(contracted)[:, None] / contracted
    kernel = np.ones_like(spacing)
    for order in range(1, contracted // 2):
        kernel = kernel + 2.0 * np.cos(2.0 * np.pi * order * spacing)
    kernel = kernel + np.cos(np.pi * contracted * spacing)
    return basis, freq, kernel / beads


def step_tables(beads, contracted):
    basis, freq, contract = cycle_tables(beads, contracted)
    step = 0.5 * TIME_STEP
    moving = freq > 0.0
    safe = np.where(moving, freq, 1.0)
    cos = np.where(moving, np.cos(safe * step), 1.0)
    sin_over = np.where(moving, np.sin(safe * step) / safe, step)
    sin_times = np.where(moving, np.sin(safe * step) * safe, 0.0)
    keep = np.exp(-np.where(moving, 2.0 * freq, CENTROID_FRICTION) * TIME_STEP)
    kick = np.sqrt(1.0 - keep * keep)

    def both(diag):
        return (basis * diag[None, :]) @ basis.T

    q_rows = np.concatenate(
        [
            both(cos * cos - keep * sin_over * sin_times),
            both(cos * sin_over * (1.0 + keep)),
            basis * (sin_over * kick)[None, :],
        ],
        axis=1,
    )
    p_rows = np.concatenate(
        [
            both(-cos * sin_times * (1.0 + keep)),
            both(cos * cos * keep - sin_over * sin_times),
            basis * (cos * kick)[None, :],
        ],
        axis=1,
    )
    return np.concatenate([q_rows, p_rows, contract @ q_rows], axis=0), contract


def split_table(table):
    table = jnp.asarray(table.astype(np.float32))
    high = table.astype(jnp.bfloat16)
    low = (table - high.astype(jnp.float32)).astype(jnp.bfloat16)
    return high, low


def dot32(left, right):
    return jnp.dot(left, right, preferred_element_type=jnp.float32)


def table_dot(high, low, x):
    x_high = x.astype(jnp.bfloat16)
    x_low = (x - x_high.astype(jnp.float32)).astype(jnp.bfloat16)
    return dot32(high, x_high) + (dot32(high, x_low) + dot32(low, x_high))


def gather_near(rows, low, first, third):
    got = [
        jnp.take_along_axis(
            jnp.broadcast_to(row, low.shape), low, axis=1, mode="promise_in_bounds"
        )
        for row in rows
    ]
    return jnp.where(first, got[0], jnp.where(third, got[2], got[1])) - rows[1]


def tile_lists(list_ref, tile, group):
    lanes = pl.ds(pl.multiple_of(tile * LANE, LANE), LANE)
    index = list_ref[8 * group : 8 * group + 8, lanes] - tile * LANE
    return index & (LANE - 1), index < LANE, index >= 2 * LANE


def closeness(apart, scale):
    return scale / (1.0 + (apart[0] * apart[0] + apart[1] * apart[1] + apart[2] * apart[2]))


def kernel(
    groups,
    q_hbm,
    n_hbm,
    p_hbm,
    f_hbm,
    mass_hbm,
    list_hbm,
    desc_hbm,
    one_hbm,
    two_hbm,
    three_hbm,
    out_w_hbm,
    perm_hbm,
    w_high_hbm,
    w_low_hbm,
    s_high_hbm,
    s_low_hbm,
    out_q,
    out_m,
    out_f,
    p_ref,
    f_ref,
    mass_ref,
    two_ref,
    three_ref,
    out_w_ref,
    perm_ref,
    w_high,
    w_low,
    s_high,
    s_low,
    sent,
    recv_in,
    xs,
    y_buf,
    back,
    ext,
    neural,
    s_buf,
    s_recv,
    edge_buf,
    pair_buf,
    lists,
    desc,
    desc_p,
    one,
    two_t,
    three_t,
    env_buf,
    layer_buf,
    local_sem,
    own_sem,
    in_send,
    in_recv,
    y_send,
    y_recv,
    s_send,
    s_recv_sem,
    halo_send,
    halo_recv,
    edge_send,
    edge_recv,
    relay_send,
    relay_recv,
):
    nb = groups
    bl = p_ref.shape[1]
    last = p_ref.shape[2]
    block = p_ref.shape[2] // nb
    tiles = p_ref.shape[2] // LANE
    wide = block // LANE
    beads = nb * bl
    nc = ext.shape[1]
    me = lax.axis_index("bead")
    slabs, cores = lax.axis_size("slab"), lax.axis_size("grp")
    total = slabs * cores
    slab = lax.axis_index("slab") * cores + lax.axis_index("grp")

    def device(place, at):
        return {"bead": place, "slab": at // cores, "grp": at % cores}


    def block_of(place, at=slab):
        if nb != 16:
            return place
        core, shift = at % cores, (3 * (at // cores)) % 4
        x, z = (place // 4 + 4 - shift) % 4, place % 4
        along_x = 4 * z + x + (z % 2) * (3 - 2 * x)
        along_z = 4 * x + 3 - z + (x % 2) * (2 * z - 3)
        return along_x + core * (along_z - along_x)

    def place_of(number, at):
        if nb != 16:
            return number
        core, shift = at % cores, (3 * (at // cores)) % 4
        far, near = number // 4, number % 4
        x_first = 4 * ((near + (far % 2) * (3 - 2 * near) + shift) % 4) + far
        z_first = 4 * ((far + shift) % 4) + 3 - near + (far % 2) * (2 * near - 3)
        return x_first + core * (z_first - x_first)

    mine = block_of(me)

    def beside(step):
        number = mine + step + nb
        at = (slab + total + number // nb - 1) % total
        return device(place_of(number % nb, at), at)

    after, before = beside(1), beside(-1)

    moves = (
        (p_hbm, p_ref),
        (f_hbm, f_ref),
        (q_hbm, sent.at[0]),
        (n_hbm, sent.at[2]),
        (desc_hbm, desc),
        (perm_hbm, perm_ref),
        (mass_hbm, mass_ref),
        (w_high_hbm, w_high),
        (w_low_hbm, w_low),
        (list_hbm, lists),
        (one_hbm, one),
        (two_hbm, two_ref),
        (three_hbm, three_ref),
        (out_w_hbm, out_w_ref),
        (s_high_hbm, s_high),
        (s_low_hbm, s_low),
    )
    loads = [
        pltpu.make_async_copy(source, dest, local_sem.at[at])
        for at, (source, dest) in enumerate(moves)
    ]
    for load in loads:
        load.start()

    barrier = pltpu.get_barrier_semaphore()

    def greet(off, carry):
        pl.semaphore_signal(
            barrier, inc=1, device_id=device((me + off) % nb, slab), device_id_type=MESH
        )
        return carry

    lax.fori_loop(1, nb, greet, 0)
    for other in (before, after):
        pl.semaphore_signal(barrier, inc=1, device_id=other, device_id_type=MESH)
    for load in loads[:4]:
        load.wait()
    sent[1] = p_ref[...] + 0.5 * TIME_STEP * f_ref[...]
    pl.semaphore_wait(barrier, nb - 1 + 2)

    def lanes_of(place):
        return pl.ds(pl.multiple_of(block_of(place) * block, LANE), block)

    def send_in(dest, source):
        return pltpu.make_async_remote_copy(
            src_ref=sent.at[:, :, :, lanes_of(dest)],
            dst_ref=recv_in.at[source],
            send_sem=in_send.at[dest],
            recv_sem=in_recv.at[source],
            device_id=device(dest, slab),
            device_id_type=MESH,
        )

    def start_in(off, carry):
        send_in((me + off) % nb, me).start()
        return carry

    lax.fori_loop(1, nb, start_in, 0)
    own_in = pltpu.make_async_copy(sent.at[:, :, :, lanes_of(me)], recv_in.at[me], own_sem.at[0])
    own_in.start()

    for load in loads[4:]:
        load.wait()
    desc_p[...] = dot32(desc[...], perm_ref[...]).astype(jnp.bfloat16)
    two_t[...] = jnp.transpose(two_ref[...])
    three_t[...] = jnp.transpose(three_ref[...])

    own_in.wait()

    def wait_in(off, carry):
        send_in((me + off) % nb, (me + off) % nb).wait_recv()
        return carry

    lax.fori_loop(1, nb, wait_in, 0)

    for part in range(3):
        for place in range(nb):
            for comp in range(3):
                row = part * beads + place * bl
                xs[row : row + bl, comp * block : (comp + 1) * block] = recv_in[place, part, comp]
    heavy = jnp.concatenate(
        [mass_ref[pl.ds(mine * wide + h, 1), :] for h in range(wide)] * 3, axis=1
    )
    x_all = jnp.concatenate(
        [
            xs[0:beads, :],
            xs[beads : 2 * beads, :] / heavy,
            xs[2 * beads : 3 * beads, :] / jnp.sqrt(heavy),
        ],
        axis=0,
    )
    y_all = table_dot(w_high[...], w_low[...], x_all)
    contracted = y_all[2 * beads : 2 * beads + nc]
    for comp in range(3):
        for cb in range(nc):
            ext[comp, cb, :, LANE : LANE + block] = contracted[
                cb : cb + 1, comp * block : (comp + 1) * block
            ]
    y_new = y_all[0:beads]
    y_mom = y_all[beads : 2 * beads] * heavy
    for arr, value in ((0, y_new), (1, y_mom)):
        for place in range(nb):
            for comp in range(3):
                y_buf[place, arr, comp] = value[
                    place * bl : (place + 1) * bl, comp * block : (comp + 1) * block
                ]

    far = LANE + block
    halos = [
        pltpu.make_async_remote_copy(
            src_ref=ext.at[:, :, :, pl.ds(block, LANE)],
            dst_ref=ext.at[:, :, :, pl.ds(0, LANE)],
            send_sem=halo_send.at[0],
            recv_sem=halo_recv.at[0],
            device_id=after,
            device_id_type=MESH,
        ),
        pltpu.make_async_remote_copy(
            src_ref=ext.at[:, :, :, pl.ds(LANE, LANE)],
            dst_ref=ext.at[:, :, :, pl.ds(far, LANE)],
            send_sem=halo_send.at[1],
            recv_sem=halo_recv.at[1],
            device_id=before,
            device_id_type=MESH,
        ),
    ]
    for halo in halos:
        halo.start()

    ends = ((0, 0), (1, nb - 1))

    def relay(which):
        return pltpu.make_async_remote_copy(
            src_ref=y_buf.at[:, 0, :, :, pl.ds((1 - which) * (block - LANE), LANE)],
            dst_ref=edge_buf.at[which],
            send_sem=relay_send.at[which],
            recv_sem=relay_recv.at[which],
            device_id=(after, before)[which],
            device_id_type=MESH,
        )

    def edge_lanes(which):
        return pl.ds(which * (last + LANE), LANE)

    def hand(which, dest):
        return pltpu.make_async_remote_copy(
            src_ref=edge_buf.at[which, dest],
            dst_ref=back.at[0, :, :, edge_lanes(which)],
            send_sem=edge_send.at[dest],
            recv_sem=edge_recv.at[which],
            device_id=device(dest, slab),
            device_id_type=MESH,
        )

    def keep(which):
        return pltpu.make_async_copy(
            edge_buf.at[which, me], back.at[0, :, :, edge_lanes(which)], own_sem.at[3 + which]
        )

    for which, end in ends:

        @pl.when(mine == nb - 1 - end)
        def _(which=which):
            relay(which).start()

    def back_lanes(source):
        return pl.ds(pl.multiple_of(LANE + block_of(source) * block, LANE), block)

    def send_y(dest, source):
        return pltpu.make_async_remote_copy(
            src_ref=y_buf.at[dest],
            dst_ref=back.at[:, :, :, back_lanes(source)],
            send_sem=y_send.at[dest],
            recv_sem=y_recv.at[source],
            device_id=device(dest, slab),
            device_id_type=MESH,
        )

    def start_y(off, carry):
        send_y((me + off) % nb, me).start()
        return carry

    lax.fori_loop(1, nb, start_y, 0)
    y_own = pltpu.make_async_copy(y_buf.at[me], back.at[:, :, :, back_lanes(me)], own_sem.at[1])
    y_own.start()
    for halo in halos:
        halo.wait_recv()

    width = lists.shape[0]
    for h in range(wide):
        for pair in range(width // 16):
            picks = [tile_lists(lists, mine * wide + h, 2 * pair + k) for k in range(2)]
            for cb in range(nc):
                halves = []
                for low, first, third in picks:
                    apart = []
                    for comp in range(3):
                        rows = [
                            ext[comp, cb, :, (h + k) * LANE : (h + k + 1) * LANE]
                            for k in range(3)
                        ]
                        apart.append(gather_near(rows, low, first, third))
                    halves.append(apart + [closeness(apart, 1.0)])
                for entry in range(4):
                    at = entry * width + 16 * pair
                    env_buf[
                        cb // 2,
                        at : at + 16,
                        ((cb % 2) * wide + h) * LANE : ((cb % 2) * wide + h + 1) * LANE,
                    ] = (
                        jnp.concatenate([halves[0][entry], halves[1][entry]], axis=0).astype(
                            jnp.bfloat16
                        )
                    )
    chunk = 512
    depth = one.shape[1]

    def two_contracted(step, carry):
        env = env_buf[step]
        total_one = None
        for low_at in range(0, depth, chunk):
            high_at = min(low_at + chunk, depth)
            piece = jnp.tanh(dot32(desc_p[low_at:high_at, :], env)).astype(jnp.bfloat16)
            term = dot32(one[:, low_at:high_at], piece)
            total_one = term if total_one is None else total_one + term
        layer_buf[step] = jnp.tanh(total_one).astype(jnp.bfloat16)
        return carry

    lax.fori_loop(0, nc // 2, two_contracted, 0)
    for which, end in ends:

        @pl.when(mine == end)
        def _(which=which):
            relay(which).wait_recv()

            def start_hand(off, carry):
                hand(which, (me + off) % nb).start()
                return carry

            lax.fori_loop(1, nb, start_hand, 0)
            keep(which).start()

    layers = [layer_buf[step] for step in range(nc // 2)]
    for matrix in (two_t, three_t):
        layers = [jnp.tanh(dot32(matrix[...], layer)).astype(jnp.bfloat16) for layer in layers]
    for step, layer in enumerate(layers):
        neural[step] = dot32(out_w_ref[...], layer)

    for comp in range(3):
        rows = jnp.concatenate([
                neural[cb // 2, comp : comp + 1, (cb % 2) * block : (cb % 2 + 1) * block]
                for cb in range(nc)
            ], axis=0)
        spread = table_dot(s_high[...], s_low[...], rows)
        for place in range(nb):
            s_buf[place, comp] = spread[place * bl : (place + 1) * bl, :]

    def send_s(dest, source):
        return pltpu.make_async_remote_copy(
            src_ref=s_buf.at[dest],
            dst_ref=s_recv.at[:, :, lanes_of(source)],
            send_sem=s_send.at[dest],
            recv_sem=s_recv_sem.at[source],
            device_id=device(dest, slab),
            device_id_type=MESH,
        )

    def start_s(off, carry):
        send_s((me + off) % nb, me).start()
        return carry

    lax.fori_loop(1, nb, start_s, 0)
    s_own = pltpu.make_async_copy(s_buf.at[me], s_recv.at[:, :, lanes_of(me)], own_sem.at[2])
    s_own.start()

    y_own.wait()

    def wait_y(off, carry):
        send_y((me + off) % nb, (me + off) % nb).wait_recv()
        return carry

    lax.fori_loop(1, nb, wait_y, 0)

    def one_tile(tile, carry):
        at = [pl.ds(pl.multiple_of((tile + k) * LANE, LANE), LANE) for k in range(3)]
        sums = [[None] * bl for _ in range(3)]
        for group in range(width // 8):
            low, first, third = tile_lists(lists, tile, group)
            for bead in range(bl):
                apart = []
                for comp in range(3):
                    rows = [back[0, comp, bead : bead + 1, at[k]] for k in range(3)]
                    apart.append(gather_near(rows, low, first, third))
                close = closeness(apart, PAIR_STRENGTH)
                for comp in range(3):
                    term = apart[comp] * close
                    old = sums[comp][bead]
                    sums[comp][bead] = term if old is None else old + term
        for comp in range(3):
            pair_buf[comp, :, at[0]] = jnp.concatenate(
                [jnp.sum(part, axis=0, keepdims=True) for part in sums[comp]], axis=0
            )
        return carry

    together = next(n for n in (5, 3, 2, 1) if (tiles - 2) % n == 0)

    def inner_tiles(step, carry):
        for k in range(together):
            one_tile(1 + together * step + k, carry)
        return carry

    lax.fori_loop(0, (tiles - 2) // together, inner_tiles, 0)
    for which, end in ends:

        @pl.when(mine == end)
        def _(which=which):
            keep(which).wait()

        @pl.when(mine != end)
        def _(which=which):
            hand(which, me).wait_recv()


    def outer_tile(which, carry):
        return one_tile(which * (tiles - 1), carry)

    lax.fori_loop(0, 2, outer_tile, 0)

    s_own.wait()

    def wait_s(off, carry):
        send_s((me + off) % nb, (me + off) % nb).wait_recv()
        return carry

    lax.fori_loop(1, nb, wait_s, 0)
    force = pair_buf[...] + s_recv[...]
    out_f[...] = force
    out_m[...] = back[1, :, :, LANE : LANE + last] + 0.5 * TIME_STEP * force
    out_q[...] = back[0, :, :, LANE : LANE + last]

    def drain(off, carry):
        dest = (me + off) % nb
        send_in(dest, me).wait_send()
        send_y(dest, me).wait_send()
        send_s(dest, me).wait_send()
        return carry

    lax.fori_loop(1, nb, drain, 0)
    for halo in halos:
        halo.wait_send()
    for which, end in ends:

        @pl.when(mine == nb - 1 - end)
        def _(which=which):
            relay(which).wait_send()

        @pl.when(mine == end)
        def _(which=which):
            def drain_hand(off, carry):
                hand(which, (me + off) % nb).wait_send()
                return carry

            lax.fori_loop(1, nb, drain_hand, 0)


def body(
    positions,
    momenta,
    force_old,
    noise,
    mass,
    pair_list,
    desc_w,
    hidden_one,
    hidden_two,
    hidden_three,
    out_w,
):
    nb = lax.axis_size("bead")
    bl, _, atoms = positions.shape
    beads = nb * bl
    block = atoms // nb
    width = pair_list.shape[1]
    env, wide = desc_w.shape
    hid = hidden_one.shape[1]
    table, contract = step_tables(beads, NC)
    w_high, w_low = split_table(table)
    s_high, s_low = split_table(contract.T * (beads / NC))
    perm = np.zeros((env, env), np.float32)
    for j in range(width):
        for entry in range(4):
            perm[4 * j + entry, entry * width + j] = 1.0
    perm = jnp.asarray(perm, jnp.bfloat16)

    def flip(x):
        return jnp.transpose(x, (1, 0, 2))

    out = jax.ShapeDtypeStruct((3, bl, atoms), jnp.float32)
    f32, bf16 = jnp.float32, jnp.bfloat16
    dma = pltpu.SemaphoreType.DMA
    new_q, new_m, new_f = pl.pallas_call(
        functools.partial(kernel, nb),
        out_shape=(out, out, out),
        in_specs=[pl.BlockSpec(memory_space=pltpu.HBM)] * 16,
        out_specs=(pl.BlockSpec(memory_space=pltpu.VMEM),) * 3,
        scratch_shapes=[
            pltpu.VMEM((3, bl, atoms), f32),
            pltpu.VMEM((3, bl, atoms), f32),
            pltpu.VMEM((atoms // LANE, LANE), f32),
            pltpu.VMEM((hid, hid), bf16),
            pltpu.VMEM((hid, hid), bf16),
            pltpu.VMEM((3, hid), bf16),
            pltpu.VMEM((env, env), bf16),
            pltpu.VMEM(w_high.shape, bf16),
            pltpu.VMEM(w_low.shape, bf16),
            pltpu.VMEM(s_high.shape, bf16),
            pltpu.VMEM(s_low.shape, bf16),
            pltpu.VMEM((3, 3, bl, atoms), f32),
            pltpu.VMEM((nb, 3, 3, bl, block), f32),
            pltpu.VMEM((3 * beads, 3 * block), f32),
            pltpu.VMEM((nb, 2, 3, bl, block), f32),
            pltpu.VMEM((2, 3, bl, atoms + 2 * LANE), f32),
            pltpu.VMEM((3, NC, 1, block + 2 * LANE), f32),
            pltpu.VMEM((NC // 2, 3, 2 * block), f32),
            pltpu.VMEM((nb, 3, bl, block), f32),
            pltpu.VMEM((3, bl, atoms), f32),
            pltpu.VMEM((2, nb, 3, bl, LANE), f32),
            pltpu.VMEM((3, bl, atoms), f32),
            pltpu.VMEM((width, atoms), jnp.int32),
            pltpu.VMEM((wide, env), bf16),
            pltpu.VMEM((wide, env), bf16),
            pltpu.VMEM((hid, wide), bf16),
            pltpu.VMEM((hid, hid), bf16),
            pltpu.VMEM((hid, hid), bf16),
            pltpu.VMEM((NC // 2, env, 2 * block), bf16),
            pltpu.VMEM((NC // 2, hid, 2 * block), bf16),
            dma((16,)),
            dma((5,)),
            dma((nb,)),
            dma((nb,)),
            dma((nb,)),
            dma((nb,)),
            dma((nb,)),
            dma((nb,)),
            dma((2,)),
            dma((2,)),
            dma((nb,)),
            dma((2,)),
            dma((2,)),
            dma((2,)),
        ],
        compiler_params=pltpu.CompilerParams(
            collective_id=0, has_side_effects=True, vmem_limit_bytes=50331648
        ),
    )(*[pltpu.with_memory_space_constraint(x, pltpu.HBM) for x in (

        flip(positions),
        flip(noise),
        flip(momenta),
        flip(force_old),
        mass.reshape(atoms // LANE, LANE),
        pair_list.T,
        desc_w.T,
        hidden_one.T,
        hidden_two,
        hidden_three,
        out_w.T,
        perm,
        w_high,
        w_low,
        s_high,
        s_low,
        )])
    return flip(new_q), flip(new_m), flip(new_f)


def solution(mesh):
    whole = P("bead", None, ("slab", "grp"))
    placed = (whole,) * 4 + (P(("slab", "grp")), P(("slab", "grp"), None)) + (P(),) * 5
    return jax.shard_map(
        body, mesh=mesh, in_specs=placed, out_specs=(whole,) * 3, check_vma=False
    )
```

```python
import functools

import jax
import jax.numpy as jnp
import numpy as np
from jax import lax
from jax.experimental import pallas as pl
from jax.experimental.pallas import tpu as pltpu
from jax.sharding import PartitionSpec as P

BEADS = 64
NC = 8
LANE = 128
TIME_STEP = 0.1
CYCLE_FREQ = 5.0
CENTROID_FRICTION = 1.0
PAIR_STRENGTH = 0.5
MESH = pl.DeviceIdType.MESH


def cycle_tables(beads, contracted):
    index = np.arange(beads, dtype=np.float64)
    mode = np.arange(beads)[None, :]
    angle = 2.0 * np.pi * index[:, None] * index[None, :] / beads
    half = beads // 2
    root_one = 1.0 / np.sqrt(beads)
    root_two = np.sqrt(2.0 / beads)
    alternate = np.where(np.arange(beads) % 2 == 0, 1.0, -1.0)[:, None]
    basis = np.where(
        mode == 0,
        root_one,
        np.where(
            mode < half,
            root_two * np.cos(angle),
            np.where(mode == half, root_one * alternate, root_two * np.sin(angle)),
        ),
    )
    freq = 2.0 * CYCLE_FREQ * np.sin(np.pi * index / beads)
    spacing = index[None, :] / beads - np.arange(contracted)[:, None] / contracted
    kernel = np.ones_like(spacing)
    for order in range(1, contracted // 2):
        kernel = kernel + 2.0 * np.cos(2.0 * np.pi * order * spacing)
    kernel = kernel + np.cos(np.pi * contracted * spacing)
    return basis, freq, kernel / beads


def step_tables(beads, contracted):
    basis, freq, contract = cycle_tables(beads, contracted)
    step = 0.5 * TIME_STEP
    moving = freq > 0.0
    safe = np.where(moving, freq, 1.0)
    cos = np.where(moving, np.cos(safe * step), 1.0)
    sin_over = np.where(moving, np.sin(safe * step) / safe, step)
    sin_times = np.where(moving, np.sin(safe * step) * safe, 0.0)
    keep = np.exp(-np.where(moving, 2.0 * freq, CENTROID_FRICTION) * TIME_STEP)
    kick = np.sqrt(1.0 - keep * keep)

    def both(diag):
        return (basis * diag[None, :]) @ basis.T

    q_rows = np.concatenate(
        [
            both(cos * cos - keep * sin_over * sin_times),
            both(cos * sin_over * (1.0 + keep)),
            basis * (sin_over * kick)[None, :],
        ],
        axis=1,
    )
    p_rows = np.concatenate(
        [
            both(-cos * sin_times * (1.0 + keep)),
            both(cos * cos * keep - sin_over * sin_times),
            basis * (cos * kick)[None, :],
        ],
        axis=1,
    )
    return np.concatenate([q_rows, p_rows, contract @ q_rows], axis=0), contract


def split_table(table):
    table = jnp.asarray(table.astype(np.float32))
    high = table.astype(jnp.bfloat16)
    low = (table - high.astype(jnp.float32)).astype(jnp.bfloat16)
    return high, low


def dot32(left, right):
    return jnp.dot(left, right, preferred_element_type=jnp.float32)


def table_dot(high, low, x):
    x_high = x.astype(jnp.bfloat16)
    x_low = (x - x_high.astype(jnp.float32)).astype(jnp.bfloat16)
    return dot32(high, x_high) + (dot32(high, x_low) + dot32(low, x_high))


def gather_near(rows, low, first, third):
    got = [
        jnp.take_along_axis(
            jnp.broadcast_to(row, low.shape), low, axis=1, mode="promise_in_bounds"
        )
        for row in rows
    ]
    return jnp.where(first, got[0], jnp.where(third, got[2], got[1])) - rows[1]


def tile_lists(list_ref, tile, group):
    lanes = pl.ds(pl.multiple_of(tile * LANE, LANE), LANE)
    index = list_ref[8 * group : 8 * group + 8, lanes] - tile * LANE
    return index & (LANE - 1), index < LANE, index >= 2 * LANE


def closeness(apart, scale):
    return scale / (1.0 + (apart[0] * apart[0] + apart[1] * apart[1] + apart[2] * apart[2]))


def kernel(
    groups,
    q_hbm,
    n_hbm,
    p_hbm,
    f_hbm,
    mass_hbm,
    list_hbm,
    desc_hbm,
    one_hbm,
    two_hbm,
    three_hbm,
    out_w_hbm,
    perm_hbm,
    w_high_hbm,
    w_low_hbm,
    s_high_hbm,
    s_low_hbm,
    out_q,
    out_m,
    out_f,
    p_ref,
    f_ref,
    mass_ref,
    two_ref,
    three_ref,
    out_w_ref,
    perm_ref,
    w_high,
    w_low,
    s_high,
    s_low,
    sent,
    recv_in,
    xs,
    y_buf,
    back,
    ext,
    neural,
    s_buf,
    s_recv,
    edge_buf,
    pair_buf,
    lists,
    desc,
    desc_p,
    one,
    two_t,
    three_t,
    env_buf,
    layer_buf,
    local_sem,
    own_sem,
    in_send,
    in_recv,
    y_send,
    y_recv,
    s_send,
    s_recv_sem,
    halo_send,
    halo_recv,
    edge_send,
    edge_recv,
    relay_send,
    relay_recv,
):
    nb = groups
    bl = p_ref.shape[1]
    last = p_ref.shape[2]
    block = p_ref.shape[2] // nb
    tiles = p_ref.shape[2] // LANE
    wide = block // LANE
    beads = nb * bl
    nc = ext.shape[1]
    me = lax.axis_index("bead")
    slabs, cores = lax.axis_size("slab"), lax.axis_size("grp")
    total = slabs * cores
    slab = lax.axis_index("slab") * cores + lax.axis_index("grp")

    def device(place, at):
        return {"bead": place, "slab": at // cores, "grp": at % cores}


    def block_of(place, at=slab):
        if nb != 16:
            return place
        core, shift = at % cores, (3 * (at // cores)) % 4
        x, z = (place // 4 + 4 - shift) % 4, place % 4
        along_x = 4 * z + x + (z % 2) * (3 - 2 * x)
        along_z = 4 * x + 3 - z + (x % 2) * (2 * z - 3)
        return along_x + core * (along_z - along_x)

    def place_of(number, at):
        if nb != 16:
            return number
        core, shift = at % cores, (3 * (at // cores)) % 4
        far, near = number // 4, number % 4
        x_first = 4 * ((near + (far % 2) * (3 - 2 * near) + shift) % 4) + far
        z_first = 4 * ((far + shift) % 4) + 3 - near + (far % 2) * (2 * near - 3)
        return x_first + core * (z_first - x_first)

    mine = block_of(me)

    def beside(step):
        number = mine + step + nb
        at = (slab + total + number // nb - 1) % total
        return device(place_of(number % nb, at), at)

    after, before = beside(1), beside(-1)

    moves = (
        (p_hbm, p_ref),
        (f_hbm, f_ref),
        (q_hbm, sent.at[0]),
        (n_hbm, sent.at[2]),
        (desc_hbm, desc),
        (perm_hbm, perm_ref),
        (mass_hbm, mass_ref),
        (w_high_hbm, w_high),
        (w_low_hbm, w_low),
        (list_hbm, lists),
        (one_hbm, one),
        (two_hbm, two_ref),
        (three_hbm, three_ref),
        (out_w_hbm, out_w_ref),
        (s_high_hbm, s_high),
        (s_low_hbm, s_low),
    )
    loads = [
        pltpu.make_async_copy(source, dest, local_sem.at[at])
        for at, (source, dest) in enumerate(moves)
    ]

    barrier = pltpu.get_barrier_semaphore()

    def greet(off, carry):
        pl.semaphore_signal(
            barrier, inc=1, device_id=device((me + off) % nb, slab), device_id_type=MESH
        )
        return carry

    lax.fori_loop(1, nb, greet, 0)
    for other in (before, after):
        pl.semaphore_signal(barrier, inc=1, device_id=other, device_id_type=MESH)
    for load in loads:
        load.start()
    for load in loads[:4]:
        load.wait()
    sent[1] = p_ref[...] + 0.5 * TIME_STEP * f_ref[...]
    pl.semaphore_wait(barrier, nb - 1 + 2)

    def lanes_of(place):
        return pl.ds(pl.multiple_of(block_of(place) * block, LANE), block)

    def send_in(dest, source):
        return pltpu.make_async_remote_copy(
            src_ref=sent.at[:, :, :, lanes_of(dest)],
            dst_ref=recv_in.at[source],
            send_sem=in_send.at[dest],
            recv_sem=in_recv.at[source],
            device_id=device(dest, slab),
            device_id_type=MESH,
        )

    def start_in(off, carry):
        send_in((me + off) % nb, me).start()
        return carry

    lax.fori_loop(1, nb, start_in, 0)
    own_in = pltpu.make_async_copy(sent.at[:, :, :, lanes_of(me)], recv_in.at[me], own_sem.at[0])
    own_in.start()

    for load in loads[4:]:
        load.wait()
    desc_p[...] = dot32(desc[...], perm_ref[...]).astype(jnp.bfloat16)
    two_t[...] = jnp.transpose(two_ref[...])
    three_t[...] = jnp.transpose(three_ref[...])

    own_in.wait()

    def wait_in(off, carry):
        send_in((me + off) % nb, (me + off) % nb).wait_recv()
        return carry

    lax.fori_loop(1, nb, wait_in, 0)

    for part in range(3):
        for place in range(nb):
            for comp in range(3):
                row = part * beads + place * bl
                xs[row : row + bl, comp * block : (comp + 1) * block] = recv_in[place, part, comp]
    heavy = jnp.concatenate(
        [mass_ref[pl.ds(mine * wide + h, 1), :] for h in range(wide)] * 3, axis=1
    )
    x_all = jnp.concatenate(
        [
            xs[0:beads, :],
            xs[beads : 2 * beads, :] / heavy,
            xs[2 * beads : 3 * beads, :] / jnp.sqrt(heavy),
        ],
        axis=0,
    )
    y_all = table_dot(w_high[...], w_low[...], x_all)
    contracted = y_all[2 * beads : 2 * beads + nc]
    for comp in range(3):
        for cb in range(nc):
            ext[comp, cb, :, LANE : LANE + block] = contracted[
                cb : cb + 1, comp * block : (comp + 1) * block
            ]
    y_new = y_all[0:beads]
    y_mom = y_all[beads : 2 * beads] * heavy
    for arr, value in ((0, y_new), (1, y_mom)):
        for place in range(nb):
            for comp in range(3):
                y_buf[place, arr, comp] = value[
                    place * bl : (place + 1) * bl, comp * block : (comp + 1) * block
                ]

    far = LANE + block
    halos = [
        pltpu.make_async_remote_copy(
            src_ref=ext.at[:, :, :, pl.ds(block, LANE)],
            dst_ref=ext.at[:, :, :, pl.ds(0, LANE)],
            send_sem=halo_send.at[0],
            recv_sem=halo_recv.at[0],
            device_id=after,
            device_id_type=MESH,
        ),
        pltpu.make_async_remote_copy(
            src_ref=ext.at[:, :, :, pl.ds(LANE, LANE)],
            dst_ref=ext.at[:, :, :, pl.ds(far, LANE)],
            send_sem=halo_send.at[1],
            recv_sem=halo_recv.at[1],
            device_id=before,
            device_id_type=MESH,
        ),
    ]
    for halo in halos:
        halo.start()

    ends = ((0, 0), (1, nb - 1))

    def relay(which):
        return pltpu.make_async_remote_copy(
            src_ref=y_buf.at[:, 0, :, :, pl.ds((1 - which) * (block - LANE), LANE)],
            dst_ref=edge_buf.at[which],
            send_sem=relay_send.at[which],
            recv_sem=relay_recv.at[which],
            device_id=(after, before)[which],
            device_id_type=MESH,
        )

    def edge_lanes(which):
        return pl.ds(which * (last + LANE), LANE)

    def hand(which, dest):
        return pltpu.make_async_remote_copy(
            src_ref=edge_buf.at[which, dest],
            dst_ref=back.at[0, :, :, edge_lanes(which)],
            send_sem=edge_send.at[dest],
            recv_sem=edge_recv.at[which],
            device_id=device(dest, slab),
            device_id_type=MESH,
        )

    def keep(which):
        return pltpu.make_async_copy(
            edge_buf.at[which, me], back.at[0, :, :, edge_lanes(which)], own_sem.at[3 + which]
        )

    for which, end in ends:

        @pl.when(mine == nb - 1 - end)
        def _(which=which):
            relay(which).start()

    def back_lanes(source):
        return pl.ds(pl.multiple_of(LANE + block_of(source) * block, LANE), block)

    def send_y(dest, source):
        return pltpu.make_async_remote_copy(
            src_ref=y_buf.at[dest],
            dst_ref=back.at[:, :, :, back_lanes(source)],
            send_sem=y_send.at[dest],
            recv_sem=y_recv.at[source],
            device_id=device(dest, slab),
            device_id_type=MESH,
        )

    def start_y(off, carry):
        send_y((me + off) % nb, me).start()
        return carry

    lax.fori_loop(1, nb, start_y, 0)
    y_own = pltpu.make_async_copy(y_buf.at[me], back.at[:, :, :, back_lanes(me)], own_sem.at[1])
    y_own.start()
    for halo in halos:
        halo.wait_recv()

    width = lists.shape[0]
    for h in range(wide):
        for pair in range(width // 16):
            picks = [tile_lists(lists, mine * wide + h, 2 * pair + k) for k in range(2)]
            for cb in range(nc):
                halves = []
                for low, first, third in picks:
                    apart = []
                    for comp in range(3):
                        rows = [
                            ext[comp, cb, :, (h + k) * LANE : (h + k + 1) * LANE]
                            for k in range(3)
                        ]
                        apart.append(gather_near(rows, low, first, third))
                    halves.append(apart + [closeness(apart, 1.0)])
                for entry in range(4):
                    at = entry * width + 16 * pair
                    env_buf[
                        cb // 2,
                        at : at + 16,
                        ((cb % 2) * wide + h) * LANE : ((cb % 2) * wide + h + 1) * LANE,
                    ] = (
                        jnp.concatenate([halves[0][entry], halves[1][entry]], axis=0).astype(
                            jnp.bfloat16
                        )
                    )
    chunk = 512
    depth = one.shape[1]

    def all_contracted():
        sums = [None] * 4
        for low_at in range(0, depth, chunk):
            high_at = min(low_at + chunk, depth)
            for k in range(4):
                piece = jnp.tanh(dot32(desc_p[low_at:high_at, :], env_buf[k]))
                term = dot32(one[:, low_at:high_at], piece.astype(jnp.bfloat16))
                sums[k] = term if sums[k] is None else sums[k] + term
        for k in range(4):
            layer_buf[k] = jnp.tanh(sums[k]).astype(jnp.bfloat16)

    all_contracted()
    for which, end in ends:

        @pl.when(mine == end)
        def _(which=which):
            relay(which).wait_recv()

            def start_hand(off, carry):
                hand(which, (me + off) % nb).start()
                return carry

            lax.fori_loop(1, nb, start_hand, 0)
            keep(which).start()

    layers = [layer_buf[step] for step in range(nc // 2)]
    for matrix in (two_t, three_t):
        layers = [jnp.tanh(dot32(matrix[...], layer)).astype(jnp.bfloat16) for layer in layers]
    for step, layer in enumerate(layers):
        neural[step] = dot32(out_w_ref[...], layer)

    for comp in range(3):
        rows = jnp.concatenate([
                neural[cb // 2, comp : comp + 1, (cb % 2) * block : (cb % 2 + 1) * block]
                for cb in range(nc)
            ], axis=0)
        spread = table_dot(s_high[...], s_low[...], rows)
        for place in range(nb):
            s_buf[place, comp] = spread[place * bl : (place + 1) * bl, :]

    def send_s(dest, source):
        return pltpu.make_async_remote_copy(
            src_ref=s_buf.at[dest],
            dst_ref=s_recv.at[:, :, lanes_of(source)],
            send_sem=s_send.at[dest],
            recv_sem=s_recv_sem.at[source],
            device_id=device(dest, slab),
            device_id_type=MESH,
        )

    def start_s(off, carry):
        send_s((me + off) % nb, me).start()
        return carry

    lax.fori_loop(1, nb, start_s, 0)
    s_own = pltpu.make_async_copy(s_buf.at[me], s_recv.at[:, :, lanes_of(me)], own_sem.at[2])
    s_own.start()

    y_own.wait()

    def wait_y(off, carry):
        send_y((me + off) % nb, (me + off) % nb).wait_recv()
        return carry

    lax.fori_loop(1, nb, wait_y, 0)

    def one_tile(tile, carry):
        at = [pl.ds(pl.multiple_of((tile + k) * LANE, LANE), LANE) for k in range(3)]
        sums = [[None] * bl for _ in range(3)]
        for group in range(width // 8):
            low, first, third = tile_lists(lists, tile, group)
            for bead in range(bl):
                apart = []
                for comp in range(3):
                    rows = [back[0, comp, bead : bead + 1, at[k]] for k in range(3)]
                    apart.append(gather_near(rows, low, first, third))
                close = closeness(apart, PAIR_STRENGTH)
                for comp in range(3):
                    term = apart[comp] * close
                    old = sums[comp][bead]
                    sums[comp][bead] = term if old is None else old + term
        for comp in range(3):
            pair_buf[comp, :, at[0]] = jnp.concatenate(
                [jnp.sum(part, axis=0, keepdims=True) for part in sums[comp]], axis=0
            )
        return carry

    together = next(n for n in (10, 5, 3, 2, 1) if (tiles - 2) % n == 0)

    def inner_tiles(step, carry):
        for k in range(together):
            one_tile(1 + together * step + k, carry)
        return carry

    lax.fori_loop(0, (tiles - 2) // together, inner_tiles, 0)
    for which, end in ends:

        @pl.when(mine == end)
        def _(which=which):
            keep(which).wait()

        @pl.when(mine != end)
        def _(which=which):
            hand(which, me).wait_recv()


    def outer_tile(which, carry):
        return one_tile(which * (tiles - 1), carry)

    lax.fori_loop(0, 2, outer_tile, 0)

    s_own.wait()

    def wait_s(off, carry):
        send_s((me + off) % nb, (me + off) % nb).wait_recv()
        return carry

    lax.fori_loop(1, nb, wait_s, 0)
    force = pair_buf[...] + s_recv[...]
    out_f[...] = force
    out_m[...] = back[1, :, :, LANE : LANE + last] + 0.5 * TIME_STEP * force
    out_q[...] = back[0, :, :, LANE : LANE + last]

    def drain(off, carry):
        dest = (me + off) % nb
        send_in(dest, me).wait_send()
        send_y(dest, me).wait_send()
        send_s(dest, me).wait_send()
        return carry

    lax.fori_loop(1, nb, drain, 0)
    for halo in halos:
        halo.wait_send()
    for which, end in ends:

        @pl.when(mine == nb - 1 - end)
        def _(which=which):
            relay(which).wait_send()

        @pl.when(mine == end)
        def _(which=which):
            def drain_hand(off, carry):
                hand(which, (me + off) % nb).wait_send()
                return carry

            lax.fori_loop(1, nb, drain_hand, 0)


def body(
    positions,
    momenta,
    force_old,
    noise,
    mass,
    pair_list,
    desc_w,
    hidden_one,
    hidden_two,
    hidden_three,
    out_w,
):
    nb = lax.axis_size("bead")
    bl, _, atoms = positions.shape
    beads = nb * bl
    block = atoms // nb
    width = pair_list.shape[1]
    env, wide = desc_w.shape
    hid = hidden_one.shape[1]
    table, contract = step_tables(beads, NC)
    w_high, w_low = split_table(table)
    s_high, s_low = split_table(contract.T * (beads / NC))
    perm = np.zeros((env, env), np.float32)
    for j in range(width):
        for entry in range(4):
            perm[4 * j + entry, entry * width + j] = 1.0
    perm = jnp.asarray(perm, jnp.bfloat16)

    def flip(x):
        return jnp.transpose(x, (1, 0, 2))

    out = jax.ShapeDtypeStruct((3, bl, atoms), jnp.float32)
    f32, bf16 = jnp.float32, jnp.bfloat16
    dma = pltpu.SemaphoreType.DMA
    new_q, new_m, new_f = pl.pallas_call(
        functools.partial(kernel, nb),
        out_shape=(out, out, out),
        in_specs=[pl.BlockSpec(memory_space=pltpu.HBM)] * 16,
        out_specs=(pl.BlockSpec(memory_space=pltpu.VMEM),) * 3,
        scratch_shapes=[
            pltpu.VMEM((3, bl, atoms), f32),
            pltpu.VMEM((3, bl, atoms), f32),
            pltpu.VMEM((atoms // LANE, LANE), f32),
            pltpu.VMEM((hid, hid), bf16),
            pltpu.VMEM((hid, hid), bf16),
            pltpu.VMEM((3, hid), bf16),
            pltpu.VMEM((env, env), bf16),
            pltpu.VMEM(w_high.shape, bf16),
            pltpu.VMEM(w_low.shape, bf16),
            pltpu.VMEM(s_high.shape, bf16),
            pltpu.VMEM(s_low.shape, bf16),
            pltpu.VMEM((3, 3, bl, atoms), f32),
            pltpu.VMEM((nb, 3, 3, bl, block), f32),
            pltpu.VMEM((3 * beads, 3 * block), f32),
            pltpu.VMEM((nb, 2, 3, bl, block), f32),
            pltpu.VMEM((2, 3, bl, atoms + 2 * LANE), f32),
            pltpu.VMEM((3, NC, 1, block + 2 * LANE), f32),
            pltpu.VMEM((NC // 2, 3, 2 * block), f32),
            pltpu.VMEM((nb, 3, bl, block), f32),
            pltpu.VMEM((3, bl, atoms), f32),
            pltpu.VMEM((2, nb, 3, bl, LANE), f32),
            pltpu.VMEM((3, bl, atoms), f32),
            pltpu.VMEM((width, atoms), jnp.int32),
            pltpu.VMEM((wide, env), bf16),
            pltpu.VMEM((wide, env), bf16),
            pltpu.VMEM((hid, wide), bf16),
            pltpu.VMEM((hid, hid), bf16),
            pltpu.VMEM((hid, hid), bf16),
            pltpu.VMEM((NC // 2, env, 2 * block), bf16),
            pltpu.VMEM((NC // 2, hid, 2 * block), bf16),
            dma((16,)),
            dma((5,)),
            dma((nb,)),
            dma((nb,)),
            dma((nb,)),
            dma((nb,)),
            dma((nb,)),
            dma((nb,)),
            dma((2,)),
            dma((2,)),
            dma((nb,)),
            dma((2,)),
            dma((2,)),
            dma((2,)),
        ],
        compiler_params=pltpu.CompilerParams(
            collective_id=0, has_side_effects=True, vmem_limit_bytes=50331648
        ),
    )(*[pltpu.with_memory_space_constraint(x, pltpu.HBM) for x in (

        flip(positions),
        flip(noise),
        flip(momenta),
        flip(force_old),
        mass.reshape(atoms // LANE, LANE),
        pair_list.T,
        desc_w.T,
        hidden_one.T,
        hidden_two,
        hidden_three,
        out_w.T,
        perm,
        w_high,
        w_low,
        s_high,
        s_low,
        )])
    return flip(new_q), flip(new_m), flip(new_f)


def solution(mesh):
    whole = P("bead", None, ("slab", "grp"))
    placed = (whole,) * 4 + (P(("slab", "grp")), P(("slab", "grp"), None)) + (P(),) * 5
    return jax.shard_map(
        body, mesh=mesh, in_specs=placed, out_specs=(whole,) * 3, check_vma=False
    )
```

```python
import functools

import jax
import jax.numpy as jnp
import numpy as np
from jax import lax
from jax.experimental import pallas as pl
from jax.experimental.pallas import tpu as pltpu
from jax.sharding import PartitionSpec as P

BEADS = 64
NC = 8
LANE = 128
TIME_STEP = 0.1
CYCLE_FREQ = 5.0
CENTROID_FRICTION = 1.0
PAIR_STRENGTH = 0.5
MESH = pl.DeviceIdType.MESH


def cycle_tables(beads, contracted):
    index = np.arange(beads, dtype=np.float64)
    mode = np.arange(beads)[None, :]
    angle = 2.0 * np.pi * index[:, None] * index[None, :] / beads
    half = beads // 2
    root_one = 1.0 / np.sqrt(beads)
    root_two = np.sqrt(2.0 / beads)
    alternate = np.where(np.arange(beads) % 2 == 0, 1.0, -1.0)[:, None]
    basis = np.where(
        mode == 0,
        root_one,
        np.where(
            mode < half,
            root_two * np.cos(angle),
            np.where(mode == half, root_one * alternate, root_two * np.sin(angle)),
        ),
    )
    freq = 2.0 * CYCLE_FREQ * np.sin(np.pi * index / beads)
    spacing = index[None, :] / beads - np.arange(contracted)[:, None] / contracted
    kernel = np.ones_like(spacing)
    for order in range(1, contracted // 2):
        kernel = kernel + 2.0 * np.cos(2.0 * np.pi * order * spacing)
    kernel = kernel + np.cos(np.pi * contracted * spacing)
    return basis, freq, kernel / beads


def step_tables(beads, contracted):
    basis, freq, contract = cycle_tables(beads, contracted)
    step = 0.5 * TIME_STEP
    moving = freq > 0.0
    safe = np.where(moving, freq, 1.0)
    cos = np.where(moving, np.cos(safe * step), 1.0)
    sin_over = np.where(moving, np.sin(safe * step) / safe, step)
    sin_times = np.where(moving, np.sin(safe * step) * safe, 0.0)
    keep = np.exp(-np.where(moving, 2.0 * freq, CENTROID_FRICTION) * TIME_STEP)
    kick = np.sqrt(1.0 - keep * keep)

    def both(diag):
        return (basis * diag[None, :]) @ basis.T

    q_rows = np.concatenate(
        [
            both(cos * cos - keep * sin_over * sin_times),
            both(cos * sin_over * (1.0 + keep)),
            basis * (sin_over * kick)[None, :],
        ],
        axis=1,
    )
    p_rows = np.concatenate(
        [
            both(-cos * sin_times * (1.0 + keep)),
            both(cos * cos * keep - sin_over * sin_times),
            basis * (cos * kick)[None, :],
        ],
        axis=1,
    )
    return np.concatenate([q_rows, p_rows, contract @ q_rows], axis=0), contract


def split_table(table):
    table = jnp.asarray(table.astype(np.float32))
    high = table.astype(jnp.bfloat16)
    low = (table - high.astype(jnp.float32)).astype(jnp.bfloat16)
    return high, low


def dot32(left, right):
    return jnp.dot(left, right, preferred_element_type=jnp.float32)


def table_dot(high, low, x):
    x_high = x.astype(jnp.bfloat16)
    x_low = (x - x_high.astype(jnp.float32)).astype(jnp.bfloat16)
    return dot32(high, x_high) + (dot32(high, x_low) + dot32(low, x_high))


def gather_near(rows, low, first, third):
    got = [
        jnp.take_along_axis(
            jnp.broadcast_to(row, low.shape), low, axis=1, mode="promise_in_bounds"
        )
        for row in rows
    ]
    return jnp.where(first, got[0], jnp.where(third, got[2], got[1])) - rows[1]


def tile_lists(list_ref, tile, group):
    lanes = pl.ds(pl.multiple_of(tile * LANE, LANE), LANE)
    index = list_ref[8 * group : 8 * group + 8, lanes] - tile * LANE
    return index & (LANE - 1), index < LANE, index >= 2 * LANE


def closeness(apart, scale):
    return scale / (1.0 + (apart[0] * apart[0] + apart[1] * apart[1] + apart[2] * apart[2]))


def kernel(
    groups,
    q_hbm,
    n_hbm,
    p_hbm,
    f_hbm,
    mass_hbm,
    list_hbm,
    desc_hbm,
    one_hbm,
    two_hbm,
    three_hbm,
    out_w_hbm,
    perm_hbm,
    w_high_hbm,
    w_low_hbm,
    s_high_hbm,
    s_low_hbm,
    out_q,
    out_m,
    pair_buf,
    s_recv,
    p_ref,
    f_ref,
    mass_ref,
    two_ref,
    three_ref,
    out_w_ref,
    perm_ref,
    w_high,
    w_low,
    s_high,
    s_low,
    sent,
    recv_in,
    xs,
    y_buf,
    back,
    ext,
    neural,
    s_buf,
    edge_buf,
    lists,
    desc,
    desc_p,
    one,
    two_t,
    three_t,
    env_buf,
    layer_buf,
    local_sem,
    own_sem,
    in_send,
    in_recv,
    y_send,
    y_recv,
    s_send,
    s_recv_sem,
    halo_send,
    halo_recv,
    edge_send,
    edge_recv,
    relay_send,
    relay_recv,
):
    nb = groups
    bl = p_ref.shape[1]
    last = p_ref.shape[2]
    block = p_ref.shape[2] // nb
    tiles = p_ref.shape[2] // LANE
    wide = block // LANE
    beads = nb * bl
    nc = ext.shape[1]
    me = lax.axis_index("bead")
    slabs, cores = lax.axis_size("slab"), lax.axis_size("grp")
    total = slabs * cores
    slab = lax.axis_index("slab") * cores + lax.axis_index("grp")

    def device(place, at):
        return {"bead": place, "slab": at // cores, "grp": at % cores}


    def block_of(place, at=slab):
        if nb != 16:
            return place
        core, shift = at % cores, (3 * (at // cores)) % 4
        x, z = (place // 4 + 4 - shift) % 4, place % 4
        along_x = 4 * z + x + (z % 2) * (3 - 2 * x)
        along_z = 4 * x + 3 - z + (x % 2) * (2 * z - 3)
        return along_x + core * (along_z - along_x)

    def place_of(number, at):
        if nb != 16:
            return number
        core, shift = at % cores, (3 * (at // cores)) % 4
        far, near = number // 4, number % 4
        x_first = 4 * ((near + (far % 2) * (3 - 2 * near) + shift) % 4) + far
        z_first = 4 * ((far + shift) % 4) + 3 - near + (far % 2) * (2 * near - 3)
        return x_first + core * (z_first - x_first)

    mine = block_of(me)

    def beside(step):
        number = mine + step + nb
        at = (slab + total + number // nb - 1) % total
        return device(place_of(number % nb, at), at)

    after, before = beside(1), beside(-1)

    moves = (
        (p_hbm, p_ref),
        (f_hbm, f_ref),
        (q_hbm, sent.at[0]),
        (n_hbm, sent.at[2]),
        (desc_hbm, desc),
        (perm_hbm, perm_ref),
        (mass_hbm, mass_ref),
        (w_high_hbm, w_high),
        (w_low_hbm, w_low),
        (list_hbm, lists),
        (one_hbm, one),
        (two_hbm, two_ref),
        (three_hbm, three_ref),
        (out_w_hbm, out_w_ref),
        (s_high_hbm, s_high),
        (s_low_hbm, s_low),
    )
    loads = [
        pltpu.make_async_copy(source, dest, local_sem.at[at])
        for at, (source, dest) in enumerate(moves)
    ]

    barrier = pltpu.get_barrier_semaphore()

    def greet(off, carry):
        pl.semaphore_signal(
            barrier, inc=1, device_id=device((me + off) % nb, slab), device_id_type=MESH
        )
        return carry

    lax.fori_loop(1, nb, greet, 0)
    for other in (before, after):
        pl.semaphore_signal(barrier, inc=1, device_id=other, device_id_type=MESH)
    for load in loads:
        load.start()
    for load in loads[:4]:
        load.wait()
    sent[1] = p_ref[...] + 0.5 * TIME_STEP * f_ref[...]
    pl.semaphore_wait(barrier, nb - 1 + 2)

    def lanes_of(place):
        return pl.ds(pl.multiple_of(block_of(place) * block, LANE), block)

    def send_in(dest, source):
        return pltpu.make_async_remote_copy(
            src_ref=sent.at[:, :, :, lanes_of(dest)],
            dst_ref=recv_in.at[source],
            send_sem=in_send.at[dest],
            recv_sem=in_recv.at[source],
            device_id=device(dest, slab),
            device_id_type=MESH,
        )

    def start_in(off, carry):
        send_in((me + off) % nb, me).start()
        return carry

    lax.fori_loop(1, nb, start_in, 0)
    own_in = pltpu.make_async_copy(sent.at[:, :, :, lanes_of(me)], recv_in.at[me], own_sem.at[0])
    own_in.start()

    for load in loads[4:]:
        load.wait()
    desc_p[...] = dot32(desc[...], perm_ref[...]).astype(jnp.bfloat16)
    two_t[...] = jnp.transpose(two_ref[...])
    three_t[...] = jnp.transpose(three_ref[...])

    own_in.wait()

    def wait_in(off, carry):
        send_in((me + off) % nb, (me + off) % nb).wait_recv()
        return carry

    lax.fori_loop(1, nb, wait_in, 0)

    for part in range(3):
        for place in range(nb):
            for comp in range(3):
                row = part * beads + place * bl
                xs[row : row + bl, comp * block : (comp + 1) * block] = recv_in[place, part, comp]
    heavy = jnp.concatenate(
        [mass_ref[pl.ds(mine * wide + h, 1), :] for h in range(wide)] * 3, axis=1
    )
    x_all = jnp.concatenate(
        [
            xs[0:beads, :],
            xs[beads : 2 * beads, :] / heavy,
            xs[2 * beads : 3 * beads, :] / jnp.sqrt(heavy),
        ],
        axis=0,
    )
    y_all = table_dot(w_high[...], w_low[...], x_all)
    contracted = y_all[2 * beads : 2 * beads + nc]
    for comp in range(3):
        for cb in range(nc):
            ext[comp, cb, :, LANE : LANE + block] = contracted[
                cb : cb + 1, comp * block : (comp + 1) * block
            ]
    y_new = y_all[0:beads]
    y_mom = y_all[beads : 2 * beads] * heavy
    for arr, value in ((0, y_new), (1, y_mom)):
        for place in range(nb):
            for comp in range(3):
                y_buf[place, arr, comp] = value[
                    place * bl : (place + 1) * bl, comp * block : (comp + 1) * block
                ]

    far = LANE + block
    halos = [
        pltpu.make_async_remote_copy(
            src_ref=ext.at[:, :, :, pl.ds(block, LANE)],
            dst_ref=ext.at[:, :, :, pl.ds(0, LANE)],
            send_sem=halo_send.at[0],
            recv_sem=halo_recv.at[0],
            device_id=after,
            device_id_type=MESH,
        ),
        pltpu.make_async_remote_copy(
            src_ref=ext.at[:, :, :, pl.ds(LANE, LANE)],
            dst_ref=ext.at[:, :, :, pl.ds(far, LANE)],
            send_sem=halo_send.at[1],
            recv_sem=halo_recv.at[1],
            device_id=before,
            device_id_type=MESH,
        ),
    ]
    for halo in halos:
        halo.start()

    ends = ((0, 0), (1, nb - 1))

    def relay(which):
        return pltpu.make_async_remote_copy(
            src_ref=y_buf.at[:, 0, :, :, pl.ds((1 - which) * (block - LANE), LANE)],
            dst_ref=edge_buf.at[which],
            send_sem=relay_send.at[which],
            recv_sem=relay_recv.at[which],
            device_id=(after, before)[which],
            device_id_type=MESH,
        )

    def edge_lanes(which):
        return pl.ds(which * (last + LANE), LANE)

    def hand(which, dest):
        return pltpu.make_async_remote_copy(
            src_ref=edge_buf.at[which, dest],
            dst_ref=back.at[0, :, :, edge_lanes(which)],
            send_sem=edge_send.at[dest],
            recv_sem=edge_recv.at[which],
            device_id=device(dest, slab),
            device_id_type=MESH,
        )

    def keep(which):
        return pltpu.make_async_copy(
            edge_buf.at[which, me], back.at[0, :, :, edge_lanes(which)], own_sem.at[3 + which]
        )

    for which, end in ends:

        @pl.when(mine == nb - 1 - end)
        def _(which=which):
            relay(which).start()

    def back_lanes(source):
        return pl.ds(pl.multiple_of(LANE + block_of(source) * block, LANE), block)

    def send_y(dest, source):
        return pltpu.make_async_remote_copy(
            src_ref=y_buf.at[dest],
            dst_ref=back.at[:, :, :, back_lanes(source)],
            send_sem=y_send.at[dest],
            recv_sem=y_recv.at[source],
            device_id=device(dest, slab),
            device_id_type=MESH,
        )

    def start_y(off, carry):
        send_y((me + off) % nb, me).start()
        return carry

    lax.fori_loop(1, nb, start_y, 0)
    y_own = pltpu.make_async_copy(y_buf.at[me], back.at[:, :, :, back_lanes(me)], own_sem.at[1])
    y_own.start()
    for halo in halos:
        halo.wait_recv()

    width = lists.shape[0]
    for h in range(wide):
        for pair in range(width // 16):
            picks = [tile_lists(lists, mine * wide + h, 2 * pair + k) for k in range(2)]
            for cb in range(nc):
                halves = []
                for low, first, third in picks:
                    apart = []
                    for comp in range(3):
                        rows = [
                            ext[comp, cb, :, (h + k) * LANE : (h + k + 1) * LANE]
                            for k in range(3)
                        ]
                        apart.append(gather_near(rows, low, first, third))
                    halves.append(apart + [closeness(apart, 1.0)])
                for entry in range(4):
                    at = entry * width + 16 * pair
                    env_buf[
                        cb // 2,
                        at : at + 16,
                        ((cb % 2) * wide + h) * LANE : ((cb % 2) * wide + h + 1) * LANE,
                    ] = (
                        jnp.concatenate([halves[0][entry], halves[1][entry]], axis=0).astype(
                            jnp.bfloat16
                        )
                    )
    chunk = 512
    depth = one.shape[1]

    def all_contracted():
        sums = [None] * 4
        for low_at in range(0, depth, chunk):
            high_at = min(low_at + chunk, depth)
            for k in range(4):
                piece = jnp.tanh(dot32(desc_p[low_at:high_at, :], env_buf[k]))
                term = dot32(one[:, low_at:high_at], piece.astype(jnp.bfloat16))
                sums[k] = term if sums[k] is None else sums[k] + term
        for k in range(4):
            layer_buf[k] = jnp.tanh(sums[k]).astype(jnp.bfloat16)

    all_contracted()
    for which, end in ends:

        @pl.when(mine == end)
        def _(which=which):
            relay(which).wait_recv()

            def start_hand(off, carry):
                hand(which, (me + off) % nb).start()
                return carry

            lax.fori_loop(1, nb, start_hand, 0)
            keep(which).start()

    layers = [layer_buf[step] for step in range(nc // 2)]
    for matrix in (two_t, three_t):
        layers = [jnp.tanh(dot32(matrix[...], layer)).astype(jnp.bfloat16) for layer in layers]
    for step, layer in enumerate(layers):
        neural[step] = dot32(out_w_ref[...], layer)

    for comp in range(3):
        rows = jnp.concatenate([
                neural[cb // 2, comp : comp + 1, (cb % 2) * block : (cb % 2 + 1) * block]
                for cb in range(nc)
            ], axis=0)
        spread = table_dot(s_high[...], s_low[...], rows)
        for place in range(nb):
            s_buf[place, comp] = spread[place * bl : (place + 1) * bl, :]

    def send_s(dest, source):
        return pltpu.make_async_remote_copy(
            src_ref=s_buf.at[dest],
            dst_ref=s_recv.at[:, :, lanes_of(source)],
            send_sem=s_send.at[dest],
            recv_sem=s_recv_sem.at[source],
            device_id=device(dest, slab),
            device_id_type=MESH,
        )

    def start_s(off, carry):
        send_s((me + off) % nb, me).start()
        return carry

    lax.fori_loop(1, nb, start_s, 0)
    s_own = pltpu.make_async_copy(s_buf.at[me], s_recv.at[:, :, lanes_of(me)], own_sem.at[2])
    s_own.start()

    y_own.wait()

    def wait_y(off, carry):
        send_y((me + off) % nb, (me + off) % nb).wait_recv()
        return carry

    lax.fori_loop(1, nb, wait_y, 0)

    def one_tile(tile, carry):
        at = [pl.ds(pl.multiple_of((tile + k) * LANE, LANE), LANE) for k in range(3)]
        sums = [[None] * bl for _ in range(3)]
        for group in range(width // 8):
            low, first, third = tile_lists(lists, tile, group)
            for bead in range(bl):
                apart = []
                for comp in range(3):
                    rows = [back[0, comp, bead : bead + 1, at[k]] for k in range(3)]
                    apart.append(gather_near(rows, low, first, third))
                close = closeness(apart, PAIR_STRENGTH)
                for comp in range(3):
                    term = apart[comp] * close
                    old = sums[comp][bead]
                    sums[comp][bead] = term if old is None else old + term
        for comp in range(3):
            pair_buf[comp, :, at[0]] = jnp.concatenate(
                [jnp.sum(part, axis=0, keepdims=True) for part in sums[comp]], axis=0
            )
        return carry

    together = next(n for n in (10, 5, 3, 2, 1) if (tiles - 2) % n == 0)

    def inner_tiles(step, carry):
        for k in range(together):
            one_tile(1 + together * step + k, carry)
        return carry

    lax.fori_loop(0, (tiles - 2) // together, inner_tiles, 0)
    for which, end in ends:

        @pl.when(mine == end)
        def _(which=which):
            keep(which).wait()

        @pl.when(mine != end)
        def _(which=which):
            hand(which, me).wait_recv()


    def outer_tile(which, carry):
        return one_tile(which * (tiles - 1), carry)

    lax.fori_loop(0, 2, outer_tile, 0)

    out_q[...] = back[0, :, :, LANE : LANE + last]
    out_m[...] = back[1, :, :, LANE : LANE + last]

    def drain(off, carry):
        dest = (me + off) % nb
        send_in(dest, me).wait_send()
        send_y(dest, me).wait_send()
        return carry

    lax.fori_loop(1, nb, drain, 0)
    for halo in halos:
        halo.wait_send()
    for which, end in ends:

        @pl.when(mine == nb - 1 - end)
        def _(which=which):
            relay(which).wait_send()

        @pl.when(mine == end)
        def _(which=which):
            def drain_hand(off, carry):
                hand(which, (me + off) % nb).wait_send()
                return carry

            lax.fori_loop(1, nb, drain_hand, 0)

    s_own.wait()

    def wait_s(off, carry):
        send_s((me + off) % nb, (me + off) % nb).wait_recv()
        return carry

    lax.fori_loop(1, nb, wait_s, 0)

    def drain_s(off, carry):
        send_s((me + off) % nb, me).wait_send()
        return carry

    lax.fori_loop(1, nb, drain_s, 0)


def body(
    positions,
    momenta,
    force_old,
    noise,
    mass,
    pair_list,
    desc_w,
    hidden_one,
    hidden_two,
    hidden_three,
    out_w,
):
    nb = lax.axis_size("bead")
    bl, _, atoms = positions.shape
    beads = nb * bl
    block = atoms // nb
    width = pair_list.shape[1]
    env, wide = desc_w.shape
    hid = hidden_one.shape[1]
    table, contract = step_tables(beads, NC)
    w_high, w_low = split_table(table)
    s_high, s_low = split_table(contract.T * (beads / NC))
    perm = np.zeros((env, env), np.float32)
    for j in range(width):
        for entry in range(4):
            perm[4 * j + entry, entry * width + j] = 1.0
    perm = jnp.asarray(perm, jnp.bfloat16)

    def flip(x):
        return jnp.transpose(x, (1, 0, 2))

    out = jax.ShapeDtypeStruct((3, bl, atoms), jnp.float32)
    f32, bf16 = jnp.float32, jnp.bfloat16
    dma = pltpu.SemaphoreType.DMA
    new_q, moved, pair, spread = pl.pallas_call(
        functools.partial(kernel, nb),
        out_shape=(out,) * 4,
        in_specs=[pl.BlockSpec(memory_space=pltpu.HBM)] * 16,
        out_specs=(pl.BlockSpec(memory_space=pltpu.VMEM),) * 4,
        scratch_shapes=[
            pltpu.VMEM((3, bl, atoms), f32),
            pltpu.VMEM((3, bl, atoms), f32),
            pltpu.VMEM((atoms // LANE, LANE), f32),
            pltpu.VMEM((hid, hid), bf16),
            pltpu.VMEM((hid, hid), bf16),
            pltpu.VMEM((3, hid), bf16),
            pltpu.VMEM((env, env), bf16),
            pltpu.VMEM(w_high.shape, bf16),
            pltpu.VMEM(w_low.shape, bf16),
            pltpu.VMEM(s_high.shape, bf16),
            pltpu.VMEM(s_low.shape, bf16),
            pltpu.VMEM((3, 3, bl, atoms), f32),
            pltpu.VMEM((nb, 3, 3, bl, block), f32),
            pltpu.VMEM((3 * beads, 3 * block), f32),
            pltpu.VMEM((nb, 2, 3, bl, block), f32),
            pltpu.VMEM((2, 3, bl, atoms + 2 * LANE), f32),
            pltpu.VMEM((3, NC, 1, block + 2 * LANE), f32),
            pltpu.VMEM((NC // 2, 3, 2 * block), f32),
            pltpu.VMEM((nb, 3, bl, block), f32),
            pltpu.VMEM((2, nb, 3, bl, LANE), f32),
            pltpu.VMEM((width, atoms), jnp.int32),
            pltpu.VMEM((wide, env), bf16),
            pltpu.VMEM((wide, env), bf16),
            pltpu.VMEM((hid, wide), bf16),
            pltpu.VMEM((hid, hid), bf16),
            pltpu.VMEM((hid, hid), bf16),
            pltpu.VMEM((NC // 2, env, 2 * block), bf16),
            pltpu.VMEM((NC // 2, hid, 2 * block), bf16),
            dma((16,)),
            dma((5,)),
            dma((nb,)),
            dma((nb,)),
            dma((nb,)),
            dma((nb,)),
            dma((nb,)),
            dma((nb,)),
            dma((2,)),
            dma((2,)),
            dma((nb,)),
            dma((2,)),
            dma((2,)),
            dma((2,)),
        ],
        compiler_params=pltpu.CompilerParams(
            collective_id=0, has_side_effects=True, vmem_limit_bytes=50331648
        ),
    )(*[pltpu.with_memory_space_constraint(x, pltpu.HBM) for x in (

        flip(positions),
        flip(noise),
        flip(momenta),
        flip(force_old),
        mass.reshape(atoms // LANE, LANE),
        pair_list.T,
        desc_w.T,
        hidden_one.T,
        hidden_two,
        hidden_three,
        out_w.T,
        perm,
        w_high,
        w_low,
        s_high,
        s_low,
        )])
    force = pair + spread
    return flip(new_q), flip(moved + 0.5 * TIME_STEP * force), flip(force)


def solution(mesh):
    whole = P("bead", None, ("slab", "grp"))
    placed = (whole,) * 4 + (P(("slab", "grp")), P(("slab", "grp"), None)) + (P(),) * 5
    return jax.shard_map(
        body, mesh=mesh, in_specs=placed, out_specs=(whole,) * 3, check_vma=False
    )
```
